768 devices in a mesh: row: 64 (over x, y, core), col: 12 (over z).
Axes of the slice: x: 4, y: 8, z: 12, core: 2. Of those that a mesh axis runs over, the one named last changes fastest.
Arguments:
- points: bfloat16 [786432, 256], P(('row', 'col'))
- centres: bfloat16 [2048, 256], replicated, may hold values from -1.5 to 1.5
- picks: int32 [2, 1024], replicated, may hold values from 0 to 786431, as said below
- assign_pts: int32 [786432], P(('row', 'col')), may hold values from 0 to 4095
- cand_assign: int32 [4096, 1], replicated, may hold values from 0 to 1023
Outputs:
- relative_cost: float32 [786432], P(('row', 'col'))
- new_centres: float32 [1024, 256], P('row')
The draws below stay inside these ranges and needn't reach their ends.
Inputs may be any that keep to these rules, and one draw needn't show every extreme that they name: Each row of picks holds 1024 distinct point indices; in each row the points of one device, the block of 1024 consecutive indices, appear at most 3 times, and some device appears exactly 3 times.
All inputs are finite; a program needn't handle non-finite values.
Results may differ from the reference program's by a relative error of at most 0.0005.
Values may be sent and summed in bfloat16 or wider, within the bound.
A program may use at most 32 MiB of HBM per device.

```python
import math
import jax
import jax.numpy as jnp
import numpy as np
from jax import lax

D = 256
NC0 = 2048
NSAMP = 1024
ROUNDS = 2
K_FINAL = 1024
PTS_DEV = 1024
NPTS = 786432
CAP = 3
K_CAND = 4096


def draw_points(key, part):
    device_total = NPTS // PTS_DEV
    first_key, second_key = jax.random.split(key)
    device_place = (jnp.arange(NPTS) // PTS_DEV).astype(jnp.float32)
    ramp = jnp.exp(math.log(3.0) * device_place / max(device_total - 1, 1))
    row_scale = jnp.exp(jax.random.uniform(second_key, (NPTS, 1), jnp.float32, math.log(0.5), math.log(2.0)))
    base_values = jnp.clip(jax.random.normal(first_key, (NPTS, D), jnp.float32), -6.0, 6.0)
    values = 0.0625 * ramp[:, None] * row_scale * base_values
    return values.astype(jnp.bfloat16)


def draw_picks(key, part):
    device_total = NPTS // PTS_DEV
    slot_total = device_total * CAP
    span_rows = PTS_DEV // CAP

    def one_round(round_key):
        first_key, second_key, third_key, fourth_key = jax.random.split(round_key, 4)
        full_device = jax.random.randint(first_key, (), 0, device_total)
        others = jax.random.permutation(second_key, slot_total - CAP)[:NSAMP - CAP]
        others = jnp.where(others >= full_device * CAP, others + CAP, others)
        slots = jnp.concatenate([full_device * CAP + jnp.arange(CAP), others])
        slots = slots[jax.random.permutation(fourth_key, NSAMP)]
        owner_device = slots // CAP
        within = slots % CAP
        offsets = jax.random.randint(third_key, (NSAMP,), 0, span_rows)
        return (owner_device * PTS_DEV + within * span_rows + offsets).astype(jnp.int32)
    return jax.vmap(one_round)(jax.random.split(key, ROUNDS))


def touch_ends(entries, own_key, low, largest):
    shape = entries.shape
    spot = [jax.random.randint(jax.random.fold_in(own_key, axis), (), 0, shape[axis]) for axis in range(len(shape))]
    entries = entries.at[tuple(spot)].set(low)
    longest = shape.index(max(shape))
    spot[longest] = (spot[longest] + 1) % shape[longest]
    return entries.at[tuple(spot)].set(largest)


def cumulative_ranks(amount, skew):
    loads = [(1 << 20) // math.isqrt(rank ** skew) + 1 for rank in range(1, amount + 1)]
    spread = 1 + sum(loads) // (1 << 30)
    return np.cumsum(np.array([max(1, weight // spread) for weight in loads]))


def ranked_ids(stream_key, shape, count, slope):
    table = cumulative_ranks(count, slope)
    lot = jax.random.randint(jax.random.fold_in(stream_key, 1), shape, 0, int(table[count - 1]))
    standing = jnp.searchsorted(jnp.asarray(table, jnp.int32), lot, side="right")
    return jax.random.permutation(jax.random.fold_in(stream_key, 2), count)[standing].astype(jnp.int32)


def distinct(stream_key, rows, count, top, lift):
    order = jax.random.permutation(jax.random.fold_in(stream_key, 1), count)
    favour = order
    for power in range(3):
        favour = favour * favour // count
    favour = favour * lift // count
    lots = jax.random.randint(jax.random.fold_in(stream_key, 2), (rows, count), 0, 4096) + favour
    holders = jax.random.permutation(jax.random.fold_in(stream_key, 3), rows)[jnp.arange(count) % rows]
    lots = jnp.where(jnp.arange(rows)[:, None] == holders[None, :], 1 << 14, lots)
    priority = lots * count + jnp.arange(count)
    return lax.top_k(priority.astype(jnp.int32), top)[1].astype(jnp.int32)


def bell_draw(own_key, dims, scale, bound, held_as=jnp.bfloat16):
    values = jax.random.normal(own_key, dims, jnp.float32) * scale
    return jnp.minimum(jnp.maximum(values, -bound), bound).astype(held_as)


def setup_inputs(seed: int = 0) -> dict:
    keys = jax.random.split(jax.random.key(seed), 6)
    points = draw_points(jax.random.fold_in(keys[5], 71), 0)
    centres = bell_draw(keys[1], (NC0, D), 0.1, 1.5)
    picks = draw_picks(jax.random.fold_in(keys[5], 71), 0)
    assign_pts = touch_ends(ranked_ids(keys[3], (NPTS,), K_CAND, 2), jax.random.fold_in(keys[3], 3), 0, K_CAND - 1).astype(jnp.int32)
    cand_assign = distinct(keys[4], K_CAND, K_FINAL, 1, 0)
    return dict(points=points, centres=centres, picks=picks, assign_pts=assign_pts, cand_assign=cand_assign)


def reference(points, centres, picks, assign_pts, cand_assign):
    sampled = points[picks.reshape(-1)]
    cand_table = jnp.concatenate([centres, sampled], axis=0)
    table_norms = jnp.sum(jnp.square(cand_table.astype(jnp.float32)), axis=1)

    def block_best(point_block):
        products = jnp.dot(point_block, cand_table.T, preferred_element_type=jnp.float32)
        point_norms = jnp.sum(jnp.square(point_block.astype(jnp.float32)), axis=1)
        distance = point_norms[:, None] + table_norms[None, :] - 2.0 * products
        return jnp.maximum(jnp.min(distance, axis=1), 0.0)

    best = lax.map(block_best, points.reshape(-1, PTS_DEV, D)).reshape(-1)
    total_cost = jnp.sum(best)
    relative_cost = best * NPTS / total_cost
    counts = jax.ops.segment_sum(jnp.ones((NPTS,), jnp.float32), assign_pts, num_segments=K_CAND)
    weights = 1.0 + counts
    weighted = weights[:, None] * cand_table.astype(jnp.float32)
    numerator = jax.ops.segment_sum(weighted, cand_assign[:, 0], num_segments=K_FINAL)
    denominator = jax.ops.segment_sum(weights, cand_assign[:, 0], num_segments=K_FINAL)
    return relative_cost, numerator / denominator[:, None]
```

```python
import functools
import jax
import jax.numpy as jnp
from jax import lax
from jax.experimental import pallas as pl
from jax.experimental.pallas import tpu as pltpu
from jax.sharding import PartitionSpec as P

K_FINAL = 1024
CORES = 2
CAP = 3
D = 256
F32, BF16, I32 = jnp.float32, jnp.bfloat16, jnp.int32
MESH = pl.DeviceIdType.MESH
BIG = 3.0e38
FAR = 1 << 20


def split3(value):
    high = value.astype(BF16)
    rest = value - high.astype(F32)
    middle = rest.astype(BF16)
    low = (rest - middle.astype(F32)).astype(BF16)
    return high, middle, low


def contract_last(left, right):
    return lax.dot_general(left, right, (((1,), (1,)), ((), ())), preferred_element_type=F32)


def near_first(size):
    return sorted(range(1, size), key=lambda step: (min(step, size - step), step))


def kernel(nx, ny, nz, npts,
           picks_ref, owner_ref, assign_ref, points_hbm, centres_hbm,
           cost_ref, final_ref,
           pts, pts2, cen, picked, zbuf, big, nearest, meta,
           hist, hist_x, hist_z, hist_y, counts,
           tot_x, tot_y, tot_z, local_sem,
           zs, zr, ys, yr, xs, xr, cs, cr,
           hxs, hxr, hzs, hzr, hys, hyr, has, har,
           txs, txr, tys, tyr, tzs, tzr):
    row = lax.axis_index("row")
    z = lax.axis_index("col")
    core = lax.rem(row, CORES)
    y = lax.rem(row // CORES, ny)
    x = row // (CORES * ny)
    me = row * nz + z
    slots = 2 * CAP
    rows = nz * slots
    blk = big.shape[3]
    nxc = nx * CORES

    def peer(ox=0, oy=0, oc=0, oz=0):
        px = lax.rem(x + ox, nx)
        py = lax.rem(y + oy, ny)
        pc = lax.rem(core + oc, CORES)
        return ((px * ny + py) * CORES + pc, lax.rem(z + oz, nz))

    def send(src, dst, ssem, rsem, device):
        copy = pltpu.make_async_remote_copy(
            src_ref=src, dst_ref=dst, send_sem=ssem, recv_sem=rsem,
            device_id=device, device_id_type=MESH)
        copy.start()
        return copy

    load_points = pltpu.make_async_copy(points_hbm, pts, local_sem.at[0])
    load_centres = pltpu.make_async_copy(centres_hbm, cen, local_sem.at[1])
    load_points.start()
    load_centres.start()

    xc_steps = [(ox, oc) for ox in range(nx) for oc in range(CORES) if ox or oc]
    barrier = pltpu.get_barrier_semaphore()
    peers = [peer(oz=o) for o in range(1, nz)] + [peer(oy=o) for o in range(1, ny)]
    peers += [peer(ox=ox, oc=oc) for ox, oc in xc_steps]
    for other in peers:
        pl.semaphore_signal(barrier, inc=1, device_id=other, device_id_type=MESH)

    for r in range(2):
        for b in range(8):
            picked[r * 8 + b:r * 8 + b + 1, :] = picks_ref[r:r + 1, b * 128:(b + 1) * 128]
    sub = lax.broadcasted_iota(I32, (8, 128), 0)
    lane = lax.broadcasted_iota(I32, (8, 128), 1)
    local_ids, codes = [], []
    for r in range(2):
        p = picked[r * 8:(r + 1) * 8, :]
        local = p - me * 1024
        own = (local >= 0) & (local < 1024)
        local = jnp.where(own, local, FAR)
        ids = r * 1024 + sub * 128 + lane
        code = ids * 1024 + owner_ref[16 + r * 8:24 + r * 8, :] + 1
        for s in range(CAP):
            first = jnp.min(jnp.min(local, axis=1, keepdims=True), axis=0, keepdims=True)
            hit = (local == first) & (local < FAR)
            coded = jnp.where(hit, code, 0)
            codes.append(jnp.max(jnp.max(coded, axis=1, keepdims=True), axis=0, keepdims=True))
            local_ids.append(first)
            local = jnp.where(local == first, FAR, local)
    slot_row = lax.broadcasted_iota(I32, (8, 1024), 0)
    point_lane = lax.broadcasted_iota(I32, (8, 1024), 1)
    want = jnp.full((8, 1024), FAR, I32)
    for s in range(slots):
        want = jnp.where(slot_row == s, local_ids[s], want)
    choose = jnp.where(want == point_lane, 1.0, 0.0)
    choose16 = jnp.concatenate([choose, jnp.zeros((8, 1024), F32)], axis=0).astype(BF16)
    lane1 = lax.broadcasted_iota(I32, (1, 128), 1)
    lane_dev = (lane1 * 43691) >> 18
    lane_slot = lane1 - lane_dev * slots
    code_row = jnp.zeros((1, 128), I32)
    for s in range(slots):
        code_row = jnp.where(lane_slot == s, codes[s], code_row)
    digit_a = (code_row & 255).astype(F32)
    digit_b = ((code_row >> 8) & 255).astype(F32)
    digit_c = (code_row >> 16).astype(F32)
    load_points.wait()
    load_centres.wait()
    mine = jnp.dot(choose16, pts[...], preferred_element_type=F32)[:8, :]
    slot_col = lax.broadcasted_iota(I32, (8, D), 0)
    filled = jnp.zeros((8, D), I32)
    for s in range(slots):
        filled = jnp.where(slot_col == s, jnp.broadcast_to(local_ids[s], (8, D)), filled)
    spare = jnp.broadcast_to(cen[0:16, :].astype(F32)[0:1, :], (8, D))
    mine = jnp.where(filled >= FAR, spare, mine)
    row_six = jnp.concatenate([digit_a, digit_b], axis=1)
    row_seven = jnp.concatenate([digit_c, digit_c], axis=1)
    mine = jnp.where(slot_col == slots, jnp.broadcast_to(row_six, (8, D)), mine)
    mine = jnp.where(slot_col == slots + 1, jnp.broadcast_to(row_seven, (8, D)), mine)
    zbuf[z] = mine.astype(BF16)

    pl.semaphore_wait(barrier, len(peers))

    sent = []
    zcopies = {}
    for o in near_first(nz)[::-1]:
        copy = send(zbuf.at[z], zbuf.at[z], zs.at[o], zr.at[o], peer(oz=o))
        sent.append(copy)

    acc = jnp.zeros((32, 128), F32)
    hi_iota = lax.broadcasted_iota(I32, (32, 128), 0)
    lo_iota = lax.broadcasted_iota(I32, (128, 128), 0)
    for b in range(8):
        a = assign_ref[b:b + 1, :]
        left = jnp.where(hi_iota == (a >> 7), 1.0, 0.0).astype(BF16)
        right = jnp.where(lo_iota == (a & 127), 1.0, 0.0).astype(BF16)
        acc = acc + contract_last(left, right)
    per = 32 // nxc
    for q in range(nxc):
        hist[q] = acc[q * per:(q + 1) * per, :]
    my_xc = x * CORES + core
    for ox, oc in xc_steps:
        o = ox * CORES + oc
        target = lax.rem(x + ox, nx) * CORES + lax.rem(core + oc, CORES)
        sent.append(send(hist.at[target], hist_x.at[o], hxs.at[o], hxr.at[o], peer(ox=ox, oc=oc)))

    p32 = pts[...].astype(F32)
    pts2[...] = (p32 * -2.0).astype(BF16)
    square = p32 * p32
    square_hi = square.astype(BF16)
    square_lo = (square - square_hi.astype(F32)).astype(BF16)
    ones = jnp.ones((16, D), BF16)
    norms = (contract_last(ones, square_hi) + contract_last(ones, square_lo))[0:1, :]

    def fold(block, masked):
        b32 = block.astype(F32)
        norm = jnp.sum(b32 * b32, axis=1, keepdims=True)
        if masked:
            place = lax.rem(lax.broadcasted_iota(I32, norm.shape, 0), blk)
            norm = jnp.where(place < rows, norm, BIG)
        for part in range(4):
            q = slice(part * 256, (part + 1) * 256)
            d = contract_last(block, pts2[q, :]) + norm
            least = jnp.min(d.reshape(d.shape[0] // 8, 8, 256), axis=0)
            nearest[:, q] = jnp.minimum(nearest[:, q], least)

    nearest[...] = jnp.full(nearest.shape, BIG, F32)

    def fold_centres(i, carry):
        fold(cen[pl.ds(pl.multiple_of(i * 512, 512), 512), :], False)
        return carry

    lax.fori_loop(0, cen.shape[0] // 512, fold_centres, 0)

    for o in near_first(nz):
        src = lax.rem(z + nz - o, nz)
        pltpu.make_async_remote_copy(
            src_ref=zbuf.at[src], dst_ref=zbuf.at[src], send_sem=zs.at[o], recv_sem=zr.at[o],
            device_id=peer(oz=o), device_id_type=MESH).wait_recv()
    column = jnp.concatenate([zbuf[i].astype(F32) for i in range(nz)], axis=0)
    crow = lax.broadcasted_iota(I32, column.shape, 0)
    clane = lax.broadcasted_iota(I32, column.shape, 1) & 127
    cdev = (clane * 43691) >> 18
    drop = ((crow & 7) >= slots) & ((crow >> 3) != cdev)
    column = jnp.where(drop, 0.0, column).astype(BF16)
    srow = lax.broadcasted_iota(I32, (blk, nz * 8), 0)
    scol = lax.broadcasted_iota(I32, (blk, nz * 8), 1)
    sdev = (srow * 43691) >> 18
    pick = (scol == sdev * 8 + (srow - sdev * slots)) & (srow < rows)
    pick = pick | ((srow == rows) & ((scol & 7) == slots))
    pick = pick | ((srow == rows + 1) & ((scol & 7) == slots + 1))
    packed = jnp.dot(jnp.where(pick, 1.0, 0.0).astype(BF16), column, preferred_element_type=F32)
    big[0, 0, 0] = packed.astype(BF16)

    def spread(o):
        for ox in near_first(nx):
            k = ox * ny + o
            sent.append(send(big.at[0, 0, o], big.at[0, ox, o], xs.at[k], xr.at[k], peer(ox=ox)))
        sent.append(send(big.at[0, 0, o], big.at[1, 0, o], cs.at[o], cr.at[o], peer(oc=1)))

    def arrive(dst, ssem, rsem, device):
        pltpu.make_async_remote_copy(
            src_ref=dst, dst_ref=dst, send_sem=ssem, recv_sem=rsem,
            device_id=device, device_id_type=MESH).wait_recv()

    for o in near_first(ny):
        sent.append(send(big.at[0, 0, 0], big.at[0, 0, o], ys.at[o], yr.at[o], peer(oy=o)))
    spread(0)

    total_h = hist[my_xc]
    for ox, oc in xc_steps:
        o = ox * CORES + oc
        arrive(hist_x.at[o], hxs.at[o], hxr.at[o], peer(ox=ox, oc=oc))
        total_h = total_h + hist_x[o]
    hist_z[0] = total_h
    for o in range(1, nz):
        sent.append(send(hist_z.at[0], hist_z.at[o], hzs.at[o], hzr.at[o], peer(oz=o)))

    for o in near_first(ny):
        arrive(big.at[0, 0, o], ys.at[o], yr.at[o], peer(oy=o))
        spread(o)

    def plane(c, ox):
        fold(big[c, ox].reshape(ny * blk, D), True)

    plane(0, 0)

    total_h = hist_z[0]
    for o in range(1, nz):
        arrive(hist_z.at[o], hzs.at[o], hzr.at[o], peer(oz=o))
        total_h = total_h + hist_z[o]
    hist_y[0] = total_h
    for o in range(1, ny):
        sent.append(send(hist_y.at[0], hist_y.at[o], hys.at[o], hyr.at[o], peer(oy=o)))

    for i, ox in enumerate(near_first(nx)):
        for o in [0] + near_first(ny):
            k = ox * ny + o
            arrive(big.at[0, ox, o], xs.at[k], xr.at[k], peer(ox=ox))
            sent.append(send(big.at[0, ox, o], big.at[1, ox, o], cs.at[k], cr.at[k], peer(oc=1)))
        plane(0, ox)
        if i == 0:
            total_h = hist_y[0]
            for o in range(1, ny):
                arrive(hist_y.at[o], hys.at[o], hyr.at[o], peer(oy=o))
                total_h = total_h + hist_y[o]
            counts[my_xc] = total_h
            for sx, sc in xc_steps:
                o = sx * CORES + sc
                sent.append(send(counts.at[my_xc], counts.at[my_xc], has.at[o], har.at[o],
                                 peer(ox=sx, oc=sc)))
    for ox in [0] + near_first(nx):
        for o in [0] + near_first(ny):
            k = ox * ny + o
            arrive(big.at[1, ox, o], cs.at[k], cr.at[k], peer(oc=1))
        plane(1, ox)

    best = jnp.maximum(jnp.min(nearest[...], axis=0, keepdims=True) + norms, 0.0)
    mass = jnp.sum(best, axis=1, keepdims=True)

    def stage(buf, ssem, rsem, steps, between):
        for o, device in steps:
            sent.append(send(buf.at[0], buf.at[o], ssem.at[o], rsem.at[o], device))
        between()
        result = buf[0]
        for o, device in steps:
            arrive(buf.at[o], ssem.at[o], rsem.at[o], device)
            result = result + buf[o]
        return result

    targets = row * (K_FINAL // (nx * ny * CORES)) + lax.broadcasted_iota(I32, (16, 128), 0)
    state = {}

    def product(member, table):
        parts = jnp.concatenate(split3(member), axis=0)
        out = jnp.dot(parts, table, preferred_element_type=F32)
        return out[0:16] + out[16:32] + out[32:48]

    def lloyd_centres():
        for ox, oc in xc_steps:
            o = ox * CORES + oc
            src = lax.rem(x + nx - ox, nx) * CORES + lax.rem(core + oc, CORES)
            arrive(counts.at[src], has.at[o], har.at[o], peer(ox=ox, oc=oc))
        weights = 1.0 + jnp.concatenate([counts[q] for q in range(nxc)], axis=0)
        pieces = []
        for t in range(16):
            hit = jnp.broadcast_to(owner_ref[t:t + 1, :], (16, 128)) == targets
            pieces.append(jnp.where(hit, jnp.broadcast_to(weights[t:t + 1, :], (16, 128)), 0.0))
        den = pieces[0]
        for t in range(1, 16):
            den = den + pieces[t]
        state["weights"] = weights
        state["den"] = den
        state["num"] = product(jnp.concatenate(pieces, axis=1), cen[...])

    def lloyd_slots(c):
        weights = state["weights"]
        num, den = state["num"], state["den"]
        for ox in range(nx):
            for o in range(ny):
                tail = big[c, ox, o, rows - 8:rows + 8, :].astype(F32)
                meta[0, o:o + 1, :] = tail[8:9, 0:128]
                meta[1, o:o + 1, :] = tail[8:9, 128:256]
                meta[2, o:o + 1, :] = tail[9:10, 0:128]
            code = (meta[0] + meta[1] * 256.0 + meta[2] * 65536.0).astype(I32) - 1
            valid = code >= 0
            owner = jnp.where(valid, code & 1023, -1)
            ident = jnp.where(valid, code >> 10, 0)
            high = ident >> 7
            low = ident & 127
            weight = jnp.zeros((ny, 128), F32)
            for h in range(16):
                table = jnp.broadcast_to(weights[16 + h:17 + h, :], (ny, 128))
                got = jnp.take_along_axis(table, low, axis=1)
                weight = jnp.where(high == h, got, weight)
            lanes = lax.broadcasted_iota(I32, (ny, 128), 1)
            owner = jnp.where(lanes < rows, owner, -1)
            for o in range(ny):
                hit = jnp.broadcast_to(owner[o:o + 1, :], (16, 128)) == targets
                member = jnp.where(hit, jnp.broadcast_to(weight[o:o + 1, :], (16, 128)), 0.0)
                den = den + member
                num = num + product(member[:, :blk], big[c, ox, o])
        state["num"], state["den"] = num, den

    tot_x[0] = jnp.broadcast_to(mass, (1, 128))
    xc = [(ox * CORES + oc, peer(ox=ox, oc=oc)) for ox, oc in xc_steps]
    tot_y[0] = stage(tot_x, txs, txr, xc, lloyd_centres)
    tot_z[0] = stage(tot_y, tys, tyr, [(o, peer(oy=o)) for o in range(1, ny)],
                     lambda: lloyd_slots(0))
    total = stage(tot_z, tzs, tzr, [(o, peer(oz=o)) for o in range(1, nz)],
                  lambda: lloyd_slots(1))
    den = jnp.sum(state["den"], axis=1, keepdims=True)
    final_ref[...] = state["num"] / den
    scaled = best * npts
    for b in range(8):
        cost_ref[b:b + 1, :] = scaled[:, b * 128:(b + 1) * 128] / total
    for copy in sent:
        copy.wait_send()


def shards(nx, ny, nz, points, centres, picks, assign_pts, cand_assign):
    nxc = nx * CORES
    blk = (nz * 2 * CAP + 2 + 15) // 16 * 16
    dma = pltpu.SemaphoreType.DMA
    per = 32 // nxc
    vmem = pl.BlockSpec(memory_space=pltpu.VMEM)
    hbm = pl.BlockSpec(memory_space=pl.ANY)
    scratch = [
        pltpu.VMEM(points.shape, BF16), pltpu.VMEM(points.shape, BF16),
        pltpu.VMEM(centres.shape, BF16), pltpu.VMEM((16, 128), I32),
        pltpu.VMEM((nz, 8, D), BF16), pltpu.VMEM((CORES, nx, ny, blk, D), BF16),
        pltpu.VMEM((8, 1024), F32), pltpu.VMEM((3, ny, 128), F32),
        pltpu.VMEM((nxc, per, 128), F32), pltpu.VMEM((nxc, per, 128), F32),
        pltpu.VMEM((nz, per, 128), F32), pltpu.VMEM((ny, per, 128), F32),
        pltpu.VMEM((nxc, per, 128), F32),
        pltpu.VMEM((nxc, 1, 128), F32), pltpu.VMEM((ny, 1, 128), F32),
        pltpu.VMEM((nz, 1, 128), F32), dma((2,)),
    ]
    for size in (nz, ny, nx * ny, nx * ny, nxc, nz, ny, nxc, nxc, ny, nz):
        scratch += [dma((size,)), dma((size,))]
    cost, final = pl.pallas_call(
        functools.partial(kernel, nx, ny, nz, float(1024 * nx * ny * CORES * nz)),
        out_shape=(jax.ShapeDtypeStruct((8, 128), F32), jax.ShapeDtypeStruct((16, D), F32)),
        in_specs=[vmem, vmem, vmem, hbm, hbm],
        out_specs=(vmem, vmem),
        scratch_shapes=scratch,
        compiler_params=pltpu.CompilerParams(
            collective_id=0, has_side_effects=True, vmem_limit_bytes=40 << 20),
    )(picks, cand_assign.reshape(32, 128), assign_pts.reshape(8, 128), points, centres)
    return cost.reshape(1024), final


def solution(mesh):
    nz = mesh.shape["col"]
    nx, ny = 4, mesh.shape["row"] // (4 * CORES)
    placed = (P(("row", "col"), None), P(), P(), P(("row", "col")), P())
    return jax.shard_map(
        functools.partial(shards, nx, ny, nz),
        mesh=mesh,
        in_specs=placed,
        out_specs=(P(("row", "col")), P("row", None)),
        check_vma=False,
    )
```

```python
import functools
import jax
import jax.numpy as jnp
from jax import lax
from jax.experimental import pallas as pl
from jax.experimental.pallas import tpu as pltpu
from jax.sharding import PartitionSpec as P

K_FINAL = 1024
CORES = 2
CAP = 3
D = 256
F32, BF16, I32 = jnp.float32, jnp.bfloat16, jnp.int32
MESH = pl.DeviceIdType.MESH
BIG = 3.0e38
FAR = 1 << 20


def split3(value):
    high = value.astype(BF16)
    rest = value - high.astype(F32)
    middle = rest.astype(BF16)
    low = (rest - middle.astype(F32)).astype(BF16)
    return high, middle, low


def contract_last(left, right):
    return lax.dot_general(left, right, (((1,), (1,)), ((), ())), preferred_element_type=F32)


def near_first(size):
    return sorted(range(1, size), key=lambda step: (min(step, size - step), step))


def kernel(nx, ny, nz, npts,
           picks_hbm, owner_hbm, assign_hbm, points_hbm, centres_hbm,
           cost_ref, final_ref,
           picks_ref, owner_ref, assign_ref, pts, pts2, cen, picked, zbuf, big, nearest, meta,
           hist, hist_x, hist_z, hist_y, counts,
           tot_x, tot_y, tot_z, local_sem,
           zs, zr, bs, br, cs, cr,
           hxs, hxr, hzs, hzr, hys, hyr, has, har,
           txs, txr, tys, tyr, tzs, tzr):
    row = lax.axis_index("row")
    z = lax.axis_index("col")
    core = lax.rem(row, CORES)
    y = lax.rem(row // CORES, ny)
    x = row // (CORES * ny)
    me = row * nz + z
    slots = 2 * CAP
    rows = nz * slots
    blk = big.shape[3]
    nxc = nx * CORES

    def peer(ox=0, oy=0, oc=0, oz=0):
        px = lax.rem(x + ox, nx)
        py = lax.rem(y + oy, ny)
        pc = lax.rem(core + oc, CORES)
        return ((px * ny + py) * CORES + pc, lax.rem(z + oz, nz))

    def send(src, dst, ssem, rsem, device):
        copy = pltpu.make_async_remote_copy(
            src_ref=src, dst_ref=dst, send_sem=ssem, recv_sem=rsem,
            device_id=device, device_id_type=MESH)
        copy.start()
        return copy

    loads = [pltpu.make_async_copy(src, dst, local_sem.at[i]) for i, (src, dst) in enumerate(
        [(picks_hbm, picks_ref), (owner_hbm, owner_ref), (points_hbm, pts),
         (centres_hbm, cen), (assign_hbm, assign_ref)])]
    for load in loads:
        load.start()

    xc_steps = [(ox, oc) for ox in range(nx) for oc in range(CORES) if ox or oc]
    barrier = pltpu.get_barrier_semaphore()
    peers = [peer(oz=o) for o in range(1, nz)] + [peer(oy=o) for o in range(1, ny)]
    peers += [peer(ox=ox, oc=oc) for ox, oc in xc_steps]
    for other in peers:
        pl.semaphore_signal(barrier, inc=1, device_id=other, device_id_type=MESH)

    loads[0].wait()
    loads[1].wait()
    for r in range(2):
        for b in range(8):
            picked[r * 8 + b:r * 8 + b + 1, :] = picks_ref[r:r + 1, b * 128:(b + 1) * 128]
    sub = lax.broadcasted_iota(I32, (8, 128), 0)
    lane = lax.broadcasted_iota(I32, (8, 128), 1)
    local_ids, codes = [], []
    for r in range(2):
        p = picked[r * 8:(r + 1) * 8, :]
        local = p - me * 1024
        own = (local >= 0) & (local < 1024)
        local = jnp.where(own, local, FAR)
        ids = r * 1024 + sub * 128 + lane
        code = ids * 1024 + owner_ref[16 + r * 8:24 + r * 8, :] + 1
        for s in range(CAP):
            first = jnp.min(jnp.min(local, axis=1, keepdims=True), axis=0, keepdims=True)
            hit = (local == first) & (local < FAR)
            coded = jnp.where(hit, code, 0)
            codes.append(jnp.max(jnp.max(coded, axis=1, keepdims=True), axis=0, keepdims=True))
            local_ids.append(first)
            local = jnp.where(local == first, FAR, local)
    slot_row = lax.broadcasted_iota(I32, (8, 1024), 0)
    point_lane = lax.broadcasted_iota(I32, (8, 1024), 1)
    want = jnp.full((8, 1024), FAR, I32)
    for s in range(slots):
        want = jnp.where(slot_row == s, local_ids[s], want)
    choose = jnp.where(want == point_lane, 1.0, 0.0)
    choose16 = jnp.concatenate([choose, jnp.zeros((8, 1024), F32)], axis=0).astype(BF16)
    lane1 = lax.broadcasted_iota(I32, (1, 128), 1)
    lane_dev = (lane1 * 43691) >> 18
    lane_slot = lane1 - lane_dev * slots
    code_row = jnp.zeros((1, 128), I32)
    for s in range(slots):
        code_row = jnp.where(lane_slot == s, codes[s], code_row)
    digit_a = (code_row & 255).astype(F32)
    digit_b = ((code_row >> 8) & 255).astype(F32)
    digit_c = (code_row >> 16).astype(F32)
    loads[2].wait()
    loads[3].wait()
    loads[4].wait()
    mine = jnp.dot(choose16, pts[...], preferred_element_type=F32)[:8, :]
    slot_col = lax.broadcasted_iota(I32, (8, D), 0)
    filled = jnp.zeros((8, D), I32)
    for s in range(slots):
        filled = jnp.where(slot_col == s, jnp.broadcast_to(local_ids[s], (8, D)), filled)
    spare = jnp.broadcast_to(cen[0:16, :].astype(F32)[0:1, :], (8, D))
    mine = jnp.where(filled >= FAR, spare, mine)
    row_six = jnp.concatenate([digit_a, digit_b], axis=1)
    row_seven = jnp.concatenate([digit_c, digit_c], axis=1)
    mine = jnp.where(slot_col == slots, jnp.broadcast_to(row_six, (8, D)), mine)
    mine = jnp.where(slot_col == slots + 1, jnp.broadcast_to(row_seven, (8, D)), mine)
    zbuf[z] = mine.astype(BF16)

    pl.semaphore_wait(barrier, len(peers))

    sent = []
    for o in near_first(nz)[::-1]:
        copy = send(zbuf.at[z], zbuf.at[z], zs.at[o], zr.at[o], peer(oz=o))
        sent.append(copy)

    acc = jnp.zeros((32, 128), F32)
    hi_iota = lax.broadcasted_iota(I32, (32, 128), 0)
    lo_iota = lax.broadcasted_iota(I32, (128, 128), 0)
    for b in range(8):
        a = assign_ref[b:b + 1, :]
        left = jnp.where(hi_iota == (a >> 7), 1.0, 0.0).astype(BF16)
        right = jnp.where(lo_iota == (a & 127), 1.0, 0.0).astype(BF16)
        acc = acc + contract_last(left, right)
    per = 32 // nxc
    for q in range(nxc):
        hist[q] = acc[q * per:(q + 1) * per, :]
    my_xc = x * CORES + core
    for ox, oc in xc_steps:
        o = ox * CORES + oc
        target = lax.rem(x + ox, nx) * CORES + lax.rem(core + oc, CORES)
        sent.append(send(hist.at[target], hist_x.at[o], hxs.at[o], hxr.at[o], peer(ox=ox, oc=oc)))

    p32 = pts[...].astype(F32)
    pts2[...] = (p32 * -2.0).astype(BF16)
    square = p32 * p32
    square_hi = square.astype(BF16)
    square_lo = (square - square_hi.astype(F32)).astype(BF16)
    ones = jnp.ones((16, D), BF16)
    norms = (contract_last(ones, square_hi) + contract_last(ones, square_lo))[0:1, :]

    def fold(block, masked):
        b32 = block.astype(F32)
        norm = jnp.sum(b32 * b32, axis=1, keepdims=True)
        if masked:
            place = lax.rem(lax.broadcasted_iota(I32, norm.shape, 0), blk)
            norm = jnp.where(place < rows, norm, BIG)
        for part in range(4):
            q = slice(part * 256, (part + 1) * 256)
            d = contract_last(block, pts2[q, :]) + norm
            least = jnp.min(d.reshape(d.shape[0] // 8, 8, 256), axis=0)
            nearest[:, q] = jnp.minimum(nearest[:, q], least)

    nearest[...] = jnp.full(nearest.shape, BIG, F32)

    def fold_centres(i, carry):
        fold(cen[pl.ds(pl.multiple_of(i * 512, 512), 512), :], False)
        return carry

    lax.fori_loop(0, cen.shape[0] // 512, fold_centres, 0)

    for o in near_first(nz):
        src = lax.rem(z + nz - o, nz)
        pltpu.make_async_remote_copy(
            src_ref=zbuf.at[src], dst_ref=zbuf.at[src], send_sem=zs.at[o], recv_sem=zr.at[o],
            device_id=peer(oz=o), device_id_type=MESH).wait_recv()
    column = jnp.concatenate([zbuf[i].astype(F32) for i in range(nz)], axis=0)
    crow = lax.broadcasted_iota(I32, column.shape, 0)
    clane = lax.broadcasted_iota(I32, column.shape, 1) & 127
    cdev = (clane * 43691) >> 18
    drop = ((crow & 7) >= slots) & ((crow >> 3) != cdev)
    column = jnp.where(drop, 0.0, column).astype(BF16)
    srow = lax.broadcasted_iota(I32, (blk, nz * 8), 0)
    scol = lax.broadcasted_iota(I32, (blk, nz * 8), 1)
    sdev = (srow * 43691) >> 18
    pick = (scol == sdev * 8 + (srow - sdev * slots)) & (srow < rows)
    pick = pick | ((srow == rows) & ((scol & 7) == slots))
    pick = pick | ((srow == rows + 1) & ((scol & 7) == slots + 1))
    packed = jnp.dot(jnp.where(pick, 1.0, 0.0).astype(BF16), column, preferred_element_type=F32)
    big[0, 0, 0] = packed.astype(BF16)

    def arrive(dst, ssem, rsem, device):
        pltpu.make_async_remote_copy(
            src_ref=dst, dst_ref=dst, send_sem=ssem, recv_sem=rsem,
            device_id=device, device_id_type=MESH).wait_recv()

    def forward(o, ox, to_o, to_ox, device):
        k = to_o * nx + to_ox
        sent.append(send(big.at[0, o, ox], big.at[0, to_o, to_ox], bs.at[k], br.at[k], device))

    def swap(o, ox):
        k = o * nx + ox
        sent.append(send(big.at[0, o, ox], big.at[1, o, ox], cs.at[k], cr.at[k], peer(oc=1)))

    def sideways(o, ox):
        if o == 0 or o == 2:
            forward(o, ox, o + 1, ox, peer(oy=1))
        if o == 0 or o == ny - 2:
            forward(o, ox, (o + ny - 1) % ny, ox, peer(oy=ny - 1))

    def landed(o, ox):
        k = o * nx + ox
        arrive(big.at[0, o, ox], bs.at[k], br.at[k], peer(oy=1))

    def swapped(o):
        for ox in range(nx):
            k = o * nx + ox
            arrive(big.at[1, o, ox], cs.at[k], cr.at[k], peer(oc=1))

    def unit(c, o):
        fold(big[c, o].reshape(nx * blk, D), True)

    xs = near_first(nx)
    far_y = (2, ny - 2, 4)
    for o in far_y:
        forward(0, 0, o, 0, peer(oy=o))
    for ox in xs:
        forward(0, 0, 0, ox, peer(ox=ox))
    sideways(0, 0)
    swap(0, 0)

    total_h = hist[my_xc]
    for ox, oc in xc_steps:
        o = ox * CORES + oc
        arrive(hist_x.at[o], hxs.at[o], hxr.at[o], peer(ox=ox, oc=oc))
        total_h = total_h + hist_x[o]
    hist_z[0] = total_h
    for o in range(1, nz):
        sent.append(send(hist_z.at[0], hist_z.at[o], hzs.at[o], hzr.at[o], peer(oz=o)))

    for o in (1, ny - 1):
        landed(o, 0)
        swap(o, 0)
    for ox in xs:
        landed(0, ox)
        sideways(0, ox)
        swap(0, ox)
    for o in far_y:
        landed(o, 0)
        for ox in xs:
            forward(o, 0, o, ox, peer(ox=ox))
        sideways(o, 0)
        swap(o, 0)
    unit(0, 0)

    total_h = hist_z[0]
    for o in range(1, nz):
        arrive(hist_z.at[o], hzs.at[o], hzr.at[o], peer(oz=o))
        total_h = total_h + hist_z[o]
    hist_y[0] = total_h
    for o in range(1, ny):
        sent.append(send(hist_y.at[0], hist_y.at[o], hys.at[o], hyr.at[o], peer(oy=o)))

    for o in (1, ny - 1):
        for ox in xs:
            landed(o, ox)
            swap(o, ox)
    swapped(0)
    unit(1, 0)
    for o in (3, ny - 3):
        landed(o, 0)
        swap(o, 0)
    unit(0, 1)
    for o in far_y[:2]:
        for ox in xs:
            landed(o, ox)
            sideways(o, ox)
            swap(o, ox)
    unit(0, ny - 1)
    for ox in xs:
        landed(4, ox)
        swap(4, ox)
    unit(0, 2)
    swapped(1)
    unit(1, 1)

    total_h = hist_y[0]
    for o in range(1, ny):
        arrive(hist_y.at[o], hys.at[o], hyr.at[o], peer(oy=o))
        total_h = total_h + hist_y[o]
    counts[my_xc] = total_h
    for ox, oc in xc_steps:
        o = ox * CORES + oc
        sent.append(send(counts.at[my_xc], counts.at[my_xc], has.at[o], har.at[o], peer(ox=ox, oc=oc)))

    unit(0, ny - 2)
    swapped(ny - 1)
    unit(1, ny - 1)
    unit(0, 4)
    for o in (3, ny - 3):
        for ox in xs:
            landed(o, ox)
            swap(o, ox)
    for o in far_y:
        swapped(o)
        unit(1, o)
    for o in (3, ny - 3):
        unit(0, o)
    for o in (3, ny - 3):
        swapped(o)
        unit(1, o)

    best = jnp.maximum(jnp.min(nearest[...], axis=0, keepdims=True) + norms, 0.0)
    mass = jnp.sum(best, axis=1, keepdims=True)

    def stage(buf, ssem, rsem, steps, between):
        for o, device in steps:
            sent.append(send(buf.at[0], buf.at[o], ssem.at[o], rsem.at[o], device))
        between()
        result = buf[0]
        for o, device in steps:
            arrive(buf.at[o], ssem.at[o], rsem.at[o], device)
            result = result + buf[o]
        return result

    targets = row * (K_FINAL // (nx * ny * CORES)) + lax.broadcasted_iota(I32, (16, 128), 0)
    state = {}

    def product(member, table):
        parts = jnp.concatenate(split3(member), axis=0)
        out = jnp.dot(parts, table, preferred_element_type=F32)
        return out[0:16] + out[16:32] + out[32:48]

    def lloyd_centres():
        for ox, oc in xc_steps:
            o = ox * CORES + oc
            src = lax.rem(x + nx - ox, nx) * CORES + lax.rem(core + oc, CORES)
            arrive(counts.at[src], has.at[o], har.at[o], peer(ox=ox, oc=oc))
        weights = 1.0 + jnp.concatenate([counts[q] for q in range(nxc)], axis=0)
        pieces = []
        for t in range(16):
            hit = jnp.broadcast_to(owner_ref[t:t + 1, :], (16, 128)) == targets
            pieces.append(jnp.where(hit, jnp.broadcast_to(weights[t:t + 1, :], (16, 128)), 0.0))
        den = pieces[0]
        for t in range(1, 16):
            den = den + pieces[t]
        state["weights"] = weights
        state["den"] = den
        state["num"] = product(jnp.concatenate(pieces, axis=1), cen[...])

    def lloyd_slots(c):
        weights = state["weights"]
        num, den = state["num"], state["den"]
        for ox in range(nx):
            for o in range(ny):
                tail = big[c, o, ox, rows - 8:rows + 8, :].astype(F32)
                meta[0, o:o + 1, :] = tail[8:9, 0:128]
                meta[1, o:o + 1, :] = tail[8:9, 128:256]
                meta[2, o:o + 1, :] = tail[9:10, 0:128]
            code = (meta[0] + meta[1] * 256.0 + meta[2] * 65536.0).astype(I32) - 1
            valid = code >= 0
            owner = jnp.where(valid, code & 1023, -1)
            ident = jnp.where(valid, code >> 10, 0)
            high = ident >> 7
            low = ident & 127
            weight = jnp.zeros((ny, 128), F32)
            for h in range(16):
                table = jnp.broadcast_to(weights[16 + h:17 + h, :], (ny, 128))
                got = jnp.take_along_axis(table, low, axis=1)
                weight = jnp.where(high == h, got, weight)
            lanes = lax.broadcasted_iota(I32, (ny, 128), 1)
            owner = jnp.where(lanes < rows, owner, -1)
            for o in range(ny):
                hit = jnp.broadcast_to(owner[o:o + 1, :], (16, 128)) == targets
                member = jnp.where(hit, jnp.broadcast_to(weight[o:o + 1, :], (16, 128)), 0.0)
                den = den + member
                num = num + product(member[:, :blk], big[c, o, ox])
        state["num"], state["den"] = num, den

    tot_x[0] = jnp.broadcast_to(mass, (1, 128))
    xc = [(ox * CORES + oc, peer(ox=ox, oc=oc)) for ox, oc in xc_steps]
    tot_y[0] = stage(tot_x, txs, txr, xc, lloyd_centres)
    tot_z[0] = stage(tot_y, tys, tyr, [(o, peer(oy=o)) for o in range(1, ny)],
                     lambda: lloyd_slots(0))
    total = stage(tot_z, tzs, tzr, [(o, peer(oz=o)) for o in range(1, nz)],
                  lambda: lloyd_slots(1))
    den = jnp.sum(state["den"], axis=1, keepdims=True)
    final_ref[...] = state["num"] / den
    scaled = best * npts
    for b in range(8):
        cost_ref[b:b + 1, :] = scaled[:, b * 128:(b + 1) * 128] / total
    for copy in sent:
        copy.wait_send()


def shards(nx, ny, nz, points, centres, picks, assign_pts, cand_assign):
    nxc = nx * CORES
    blk = (nz * 2 * CAP + 2 + 15) // 16 * 16
    dma = pltpu.SemaphoreType.DMA
    per = 32 // nxc
    vmem = pl.BlockSpec(memory_space=pltpu.VMEM)
    hbm = pl.BlockSpec(memory_space=pltpu.MemorySpace.HBM)
    scratch = [
        pltpu.VMEM(picks.shape, I32), pltpu.VMEM((32, 128), I32), pltpu.VMEM((8, 128), I32),
        pltpu.VMEM(points.shape, BF16), pltpu.VMEM(points.shape, BF16),
        pltpu.VMEM(centres.shape, BF16), pltpu.VMEM((16, 128), I32),
        pltpu.VMEM((nz, 8, D), BF16), pltpu.VMEM((CORES, ny, nx, blk, D), BF16),
        pltpu.VMEM((8, 1024), F32), pltpu.VMEM((3, ny, 128), F32),
        pltpu.VMEM((nxc, per, 128), F32), pltpu.VMEM((nxc, per, 128), F32),
        pltpu.VMEM((nz, per, 128), F32), pltpu.VMEM((ny, per, 128), F32),
        pltpu.VMEM((nxc, per, 128), F32),
        pltpu.VMEM((nxc, 1, 128), F32), pltpu.VMEM((ny, 1, 128), F32),
        pltpu.VMEM((nz, 1, 128), F32), dma((5,)),
    ]
    for size in (nz, nx * ny, nx * ny, nxc, nz, ny, nxc, nxc, ny, nz):
        scratch += [dma((size,)), dma((size,))]
    cost, final = pl.pallas_call(
        functools.partial(kernel, nx, ny, nz, float(1024 * nx * ny * CORES * nz)),
        out_shape=(jax.ShapeDtypeStruct((8, 128), F32), jax.ShapeDtypeStruct((16, D), F32)),
        in_specs=[hbm] * 5,
        out_specs=(vmem, vmem),
        scratch_shapes=scratch,
        compiler_params=pltpu.CompilerParams(
            collective_id=0, has_side_effects=True, vmem_limit_bytes=60 << 20),
    )(picks, cand_assign.reshape(32, 128), assign_pts.reshape(8, 128), points, centres)
    return cost.reshape(1024), final


def solution(mesh):
    nz = mesh.shape["col"]
    nx, ny = 4, mesh.shape["row"] // (4 * CORES)
    placed = (P(("row", "col"), None), P(), P(), P(("row", "col")), P())
    return jax.shard_map(
        functools.partial(shards, nx, ny, nz),
        mesh=mesh,
        in_specs=placed,
        out_specs=(P(("row", "col")), P("row", None)),
        check_vma=False,
    )
```

```python
import functools
import jax
import jax.numpy as jnp
from jax import lax
from jax.experimental import pallas as pl
from jax.experimental.pallas import tpu as pltpu
from jax.sharding import PartitionSpec as P

K_FINAL = 1024
CORES = 2
CAP = 3
D = 256
F32, BF16, I32 = jnp.float32, jnp.bfloat16, jnp.int32
MESH = pl.DeviceIdType.MESH
BIG = 3.0e38
FAR = 1 << 20


def split3(value):
    high = value.astype(BF16)
    rest = value - high.astype(F32)
    middle = rest.astype(BF16)
    low = (rest - middle.astype(F32)).astype(BF16)
    return high, middle, low


def contract_last(left, right):
    return lax.dot_general(left, right, (((1,), (1,)), ((), ())), preferred_element_type=F32)


def near_first(size):
    return sorted(range(1, size), key=lambda step: (min(step, size - step), step))


def kernel(nx, ny, nz, npts,
           picks_hbm, owner_hbm, assign_hbm, points_hbm, centres_hbm,
           cost_ref, final_ref,
           picks_ref, owner_ref, assign_ref, pts, pts2, cen, picked, zbuf, big, nearest, meta,
           hist, hist_x, hist_z, hist_y, counts,
           tot_x, tot_y, tot_z, local_sem, ssem, rsem, block_sem, swap_sem):
    row = lax.axis_index("row")
    z = lax.axis_index("col")
    core = lax.rem(row, CORES)
    y = lax.rem(row // CORES, ny)
    x = row // (CORES * ny)
    me = row * nz + z
    slots = 2 * CAP
    rows = nz * slots
    blk = big.shape[3]
    nxc = nx * CORES

    def peer(ox=0, oy=0, oc=0, oz=0):
        px = lax.rem(x + ox, nx)
        py = lax.rem(y + oy, ny)
        pc = lax.rem(core + oc, CORES)
        return ((px * ny + py) * CORES + pc, lax.rem(z + oz, nz))

    def send(src, dst, out_sem, in_sem, device):
        pltpu.make_async_remote_copy(
            src_ref=src, dst_ref=dst, send_sem=out_sem, recv_sem=in_sem,
            device_id=device, device_id_type=MESH).start()

    def waiter(ref, sem):
        return pltpu.make_async_remote_copy(
            src_ref=ref, dst_ref=ref, send_sem=sem, recv_sem=sem,
            device_id=peer(oz=1), device_id_type=MESH)

    def arrive(ref, sem):
        waiter(ref, sem).wait_recv()

    def drain(ref, sem):
        waiter(ref, sem).wait_send()

    def others(ref, size):
        return ref.at[pl.ds(0, size - 1)]

    loads = [pltpu.make_async_copy(src, dst, local_sem.at[i]) for i, (src, dst) in enumerate(
        [(picks_hbm, picks_ref), (owner_hbm, owner_ref), (points_hbm, pts),
         (centres_hbm, cen), (assign_hbm, assign_ref)])]
    for load in loads:
        load.start()

    xc_steps = [(ox, oc) for ox in range(nx) for oc in range(CORES) if ox or oc]
    barrier = pltpu.get_barrier_semaphore()
    peers = [peer(oz=o) for o in range(1, nz)] + [peer(oy=o) for o in range(1, ny)]
    peers += [peer(ox=ox, oc=oc) for ox, oc in xc_steps]
    for other in peers:
        pl.semaphore_signal(barrier, inc=1, device_id=other, device_id_type=MESH)

    loads[0].wait()
    loads[1].wait()
    for r in range(2):
        for b in range(8):
            picked[r * 8 + b:r * 8 + b + 1, :] = picks_ref[r:r + 1, b * 128:(b + 1) * 128]
    sub = lax.broadcasted_iota(I32, (8, 128), 0)
    lane = lax.broadcasted_iota(I32, (8, 128), 1)
    local_ids, codes = [], []
    for r in range(2):
        p = picked[r * 8:(r + 1) * 8, :]
        local = p - me * 1024
        own = (local >= 0) & (local < 1024)
        local = jnp.where(own, local, FAR)
        ids = r * 1024 + sub * 128 + lane
        code = ids * 1024 + owner_ref[16 + r * 8:24 + r * 8, :] + 1
        for s in range(CAP):
            first = jnp.min(jnp.min(local, axis=1, keepdims=True), axis=0, keepdims=True)
            hit = (local == first) & (local < FAR)
            coded = jnp.where(hit, code, 0)
            codes.append(jnp.max(jnp.max(coded, axis=1, keepdims=True), axis=0, keepdims=True))
            local_ids.append(first)
            local = jnp.where(local == first, FAR, local)
    slot_row = lax.broadcasted_iota(I32, (8, 1024), 0)
    point_lane = lax.broadcasted_iota(I32, (8, 1024), 1)
    want = jnp.full((8, 1024), FAR, I32)
    for s in range(slots):
        want = jnp.where(slot_row == s, local_ids[s], want)
    choose = jnp.where(want == point_lane, 1.0, 0.0)
    choose16 = jnp.concatenate([choose, jnp.zeros((8, 1024), F32)], axis=0).astype(BF16)
    lane1 = lax.broadcasted_iota(I32, (1, 128), 1)
    lane_dev = (lane1 * 43691) >> 18
    lane_slot = lane1 - lane_dev * slots
    code_row = jnp.zeros((1, 128), I32)
    for s in range(slots):
        code_row = jnp.where(lane_slot == s, codes[s], code_row)
    digit_a = (code_row & 255).astype(F32)
    digit_b = ((code_row >> 8) & 255).astype(F32)
    digit_c = (code_row >> 16).astype(F32)
    loads[2].wait()
    loads[3].wait()
    loads[4].wait()
    mine = jnp.dot(choose16, pts[...], preferred_element_type=F32)[:8, :]
    slot_col = lax.broadcasted_iota(I32, (8, D), 0)
    filled = jnp.zeros((8, D), I32)
    for s in range(slots):
        filled = jnp.where(slot_col == s, jnp.broadcast_to(local_ids[s], (8, D)), filled)
    spare = jnp.broadcast_to(cen[0:16, :].astype(F32)[0:1, :], (8, D))
    mine = jnp.where(filled >= FAR, spare, mine)
    row_six = jnp.concatenate([digit_a, digit_b], axis=1)
    row_seven = jnp.concatenate([digit_c, digit_c], axis=1)
    mine = jnp.where(slot_col == slots, jnp.broadcast_to(row_six, (8, D)), mine)
    mine = jnp.where(slot_col == slots + 1, jnp.broadcast_to(row_seven, (8, D)), mine)
    zbuf[z] = mine.astype(BF16)

    pl.semaphore_wait(barrier, len(peers))

    for o in near_first(nz)[::-1]:
        send(zbuf.at[z], zbuf.at[z], ssem.at[0], rsem.at[0], peer(oz=o))

    acc = jnp.zeros((32, 128), F32)
    hi_iota = lax.broadcasted_iota(I32, (32, 128), 0)
    lo_iota = lax.broadcasted_iota(I32, (128, 128), 0)
    for b in range(8):
        a = assign_ref[b:b + 1, :]
        left = jnp.where(hi_iota == (a >> 7), 1.0, 0.0).astype(BF16)
        right = jnp.where(lo_iota == (a & 127), 1.0, 0.0).astype(BF16)
        acc = acc + contract_last(left, right)
    per = 32 // nxc
    for q in range(nxc):
        hist[q] = acc[q * per:(q + 1) * per, :]
    my_xc = x * CORES + core
    for ox, oc in xc_steps:
        o = ox * CORES + oc
        target = lax.rem(x + ox, nx) * CORES + lax.rem(core + oc, CORES)
        send(hist.at[target], hist_x.at[o], ssem.at[1], rsem.at[1], peer(ox=ox, oc=oc))

    p32 = pts[...].astype(F32)
    pts2[...] = (p32 * -2.0).astype(BF16)
    square = p32 * p32
    square_hi = square.astype(BF16)
    square_lo = (square - square_hi.astype(F32)).astype(BF16)
    ones = jnp.ones((16, D), BF16)
    norms = (contract_last(ones, square_hi) + contract_last(ones, square_lo))[0:1, :]

    def fold(block, masked):
        b32 = block.astype(F32)
        norm = jnp.sum(b32 * b32, axis=1, keepdims=True)
        if masked:
            place = lax.rem(lax.broadcasted_iota(I32, norm.shape, 0), blk)
            norm = jnp.where(place < rows, norm, BIG)
        for part in range(4):
            q = slice(part * 256, (part + 1) * 256)
            d = contract_last(block, pts2[q, :]) + norm
            least = jnp.min(d.reshape(d.shape[0] // 8, 8, 256), axis=0)
            nearest[:, q] = jnp.minimum(nearest[:, q], least)

    nearest[...] = jnp.full(nearest.shape, BIG, F32)

    def fold_centres(i, carry):
        fold(cen[pl.ds(pl.multiple_of(i * 512, 512), 512), :], False)
        return carry

    lax.fori_loop(0, cen.shape[0] // 512, fold_centres, 0)

    arrive(others(zbuf, nz), rsem.at[0])
    column = jnp.concatenate([zbuf[i].astype(F32) for i in range(nz)], axis=0)
    crow = lax.broadcasted_iota(I32, column.shape, 0)
    clane = lax.broadcasted_iota(I32, column.shape, 1) & 127
    cdev = (clane * 43691) >> 18
    drop = ((crow & 7) >= slots) & ((crow >> 3) != cdev)
    column = jnp.where(drop, 0.0, column).astype(BF16)
    srow = lax.broadcasted_iota(I32, (blk, nz * 8), 0)
    scol = lax.broadcasted_iota(I32, (blk, nz * 8), 1)
    sdev = (srow * 43691) >> 18
    pick = (scol == sdev * 8 + (srow - sdev * slots)) & (srow < rows)
    pick = pick | ((srow == rows) & ((scol & 7) == slots))
    pick = pick | ((srow == rows + 1) & ((scol & 7) == slots + 1))
    packed = jnp.dot(jnp.where(pick, 1.0, 0.0).astype(BF16), column, preferred_element_type=F32)
    big[0, 0, 0] = packed.astype(BF16)

    parity = lax.rem(z, 2)
    steps = (0, 3, 1, 2)
    xs = near_first(nx)

    def mine_of(i):
        return 2 * i + parity

    def theirs_of(i):
        return 2 * i + 1 - parity

    def slot(o, ox):
        return block_sem.at[o * nx + ox]

    def forward(o, ox, to_o, to_ox, out_sem, device):
        send(big.at[0, o, ox], big.at[0, to_o, to_ox], ssem.at[out_sem], slot(to_o, to_ox), device)

    def swap(o, ox):
        send(big.at[0, o, ox], big.at[1, o, ox], ssem.at[8], swap_sem.at[o], peer(oc=1))

    def upright(i, ox, out_sem):
        o = mine_of(i)
        forward(o, ox, o, ox, out_sem, peer(oz=1 if i < 2 else nz - 1))

    def landed(o, ox):
        arrive(big.at[0, o, ox], slot(o, ox))

    def across(i):
        o = mine_of(i)
        for ox in xs:
            forward(o, 0, o, ox, 11, peer(ox=ox))

    def from_x(i):
        for ox in xs:
            landed(mine_of(i), ox)
            upright(i, ox, 12 if i else 13)
            swap(mine_of(i), ox)

    def from_z(i):
        o = theirs_of(i)
        if i:
            landed(o, 0)
            swap(o, 0)
        else:
            @pl.when(parity == 0)
            def _():
                landed(o, 0)
                swap(o, 0)
        for ox in xs:
            landed(o, ox)
            swap(o, ox)

    def unit(c, o):
        fold(big[c, o].reshape(nx * blk, D), True)

    def swapped(o):
        arrive(big.at[1, o], swap_sem.at[o])
        unit(1, o)

    for i in (2, 1, 3):
        forward(0, 0, mine_of(i), 0, 9, peer(oy=mine_of(i)))

    @pl.when(parity == 1)
    def _():
        forward(0, 0, 1, 0, 10, peer(oy=1))

    swap(0, 0)

    arrive(others(hist_x, nxc), rsem.at[1])
    total_h = hist[my_xc]
    for o in range(1, nxc):
        total_h = total_h + hist_x[o]
    hist_z[0] = total_h

    @pl.when(parity == 1)
    def _():
        landed(1, 0)
        upright(0, 0, 14)
        swap(1, 0)

    across(0)
    for o in range(1, nz):
        send(hist_z.at[0], hist_z.at[o], ssem.at[2], rsem.at[2], peer(oz=o))
    for i in steps[1:]:
        landed(mine_of(i), 0)
        across(i)
        upright(i, 0, 12)
        swap(mine_of(i), 0)
    from_x(0)
    unit(0, mine_of(0))

    arrive(others(hist_z, nz), rsem.at[2])
    total_h = hist_z[0]
    for o in range(1, nz):
        total_h = total_h + hist_z[o]
    hist_y[0] = total_h
    for o in range(1, ny):
        send(hist_y.at[0], hist_y.at[o], ssem.at[3], rsem.at[3], peer(oy=o))

    from_x(3)
    unit(0, mine_of(3))
    from_z(0)
    swapped(mine_of(0))
    from_x(1)
    unit(0, mine_of(1))
    from_z(3)
    unit(0, theirs_of(0))
    swapped(mine_of(3))

    arrive(others(hist_y, ny), rsem.at[3])
    total_h = hist_y[0]
    for o in range(1, ny):
        total_h = total_h + hist_y[o]
    counts[my_xc] = total_h
    for ox, oc in xc_steps:
        send(counts.at[my_xc], counts.at[my_xc], ssem.at[4], rsem.at[4], peer(ox=ox, oc=oc))

    from_x(2)
    unit(0, mine_of(2))
    from_z(1)
    unit(0, theirs_of(3))
    swapped(theirs_of(0))
    swapped(mine_of(1))
    from_z(2)
    unit(0, theirs_of(1))
    swapped(theirs_of(3))
    swapped(mine_of(2))
    unit(0, theirs_of(2))
    swapped(theirs_of(1))
    swapped(theirs_of(2))

    best = jnp.maximum(jnp.min(nearest[...], axis=0, keepdims=True) + norms, 0.0)
    mass = jnp.sum(best, axis=1, keepdims=True)

    def stage(buf, sem, devices, between):
        for o, device in enumerate(devices):
            send(buf.at[0], buf.at[o + 1], ssem.at[sem], rsem.at[sem], device)
        between()
        arrive(others(buf, len(devices) + 1), rsem.at[sem])
        result = buf[0]
        for o in range(len(devices)):
            result = result + buf[o + 1]
        return result

    targets = row * (K_FINAL // (nx * ny * CORES)) + lax.broadcasted_iota(I32, (16, 128), 0)
    state = {}

    def product(member, table):
        parts = jnp.concatenate(split3(member), axis=0)
        out = jnp.dot(parts, table, preferred_element_type=F32)
        return out[0:16] + out[16:32] + out[32:48]

    def lloyd_centres():
        arrive(others(counts, nxc), rsem.at[4])
        weights = 1.0 + jnp.concatenate([counts[q] for q in range(nxc)], axis=0)
        pieces = []
        for t in range(16):
            hit = jnp.broadcast_to(owner_ref[t:t + 1, :], (16, 128)) == targets
            pieces.append(jnp.where(hit, jnp.broadcast_to(weights[t:t + 1, :], (16, 128)), 0.0))
        den = pieces[0]
        for t in range(1, 16):
            den = den + pieces[t]
        state["weights"] = weights
        state["den"] = den
        state["num"] = product(jnp.concatenate(pieces, axis=1), cen[...])

    def lloyd_slots(c):
        weights = state["weights"]
        num, den = state["num"], state["den"]
        for ox in range(nx):
            for o in range(ny):
                tail = big[c, o, ox, rows - 8:rows + 8, :].astype(F32)
                meta[0, o:o + 1, :] = tail[8:9, 0:128]
                meta[1, o:o + 1, :] = tail[8:9, 128:256]
                meta[2, o:o + 1, :] = tail[9:10, 0:128]
            code = (meta[0] + meta[1] * 256.0 + meta[2] * 65536.0).astype(I32) - 1
            valid = code >= 0
            owner = jnp.where(valid, code & 1023, -1)
            ident = jnp.where(valid, code >> 10, 0)
            high = ident >> 7
            low = ident & 127
            weight = jnp.zeros((ny, 128), F32)
            for h in range(16):
                table = jnp.broadcast_to(weights[16 + h:17 + h, :], (ny, 128))
                got = jnp.take_along_axis(table, low, axis=1)
                weight = jnp.where(high == h, got, weight)
            lanes = lax.broadcasted_iota(I32, (ny, 128), 1)
            owner = jnp.where(lanes < rows, owner, -1)
            for o in range(ny):
                hit = jnp.broadcast_to(owner[o:o + 1, :], (16, 128)) == targets
                member = jnp.where(hit, jnp.broadcast_to(weight[o:o + 1, :], (16, 128)), 0.0)
                den = den + member
                num = num + product(member[:, :blk], big[c, o, ox])
        state["num"], state["den"] = num, den

    tot_x[0] = jnp.broadcast_to(mass, (1, 128))
    tot_y[0] = stage(tot_x, 5, [peer(ox=ox, oc=oc) for ox, oc in xc_steps], lloyd_centres)
    tot_z[0] = stage(tot_y, 6, [peer(oy=o) for o in range(1, ny)], lambda: lloyd_slots(0))
    total = stage(tot_z, 7, [peer(oz=o) for o in range(1, nz)], lambda: lloyd_slots(1))
    den = jnp.sum(state["den"], axis=1, keepdims=True)
    final_ref[...] = state["num"] / den
    scaled = best * npts
    for b in range(8):
        cost_ref[b:b + 1, :] = scaled[:, b * 128:(b + 1) * 128] / total
    drain(others(zbuf, nz), ssem.at[0])
    drain(others(hist_x, nxc), ssem.at[1])
    drain(others(hist_z, nz), ssem.at[2])
    drain(others(hist_y, ny), ssem.at[3])
    drain(others(counts, nxc), ssem.at[4])
    drain(others(tot_x, nxc), ssem.at[5])
    drain(others(tot_y, ny), ssem.at[6])
    drain(others(tot_z, nz), ssem.at[7])
    drain(big.at[1], ssem.at[8])
    drain(big.at[0, 0, pl.ds(0, 3)], ssem.at[9])
    drain(big.at[0, pl.ds(0, nx - 1)], ssem.at[11])
    drain(big.at[0, pl.ds(0, 3)], ssem.at[12])
    drain(big.at[0, 0, pl.ds(0, nx - 1)], ssem.at[13])

    @pl.when(parity == 1)
    def _():
        drain(big.at[0, 0, 0], ssem.at[10])
        drain(big.at[0, 0, 0], ssem.at[14])


def shards(nx, ny, nz, points, centres, picks, assign_pts, cand_assign):
    nxc = nx * CORES
    blk = (nz * 2 * CAP + 2 + 15) // 16 * 16
    dma = pltpu.SemaphoreType.DMA
    per = 32 // nxc
    vmem = pl.BlockSpec(memory_space=pltpu.VMEM)
    hbm = pl.BlockSpec(memory_space=pltpu.MemorySpace.HBM)
    scratch = [
        pltpu.VMEM(picks.shape, I32), pltpu.VMEM((32, 128), I32), pltpu.VMEM((8, 128), I32),
        pltpu.VMEM(points.shape, BF16), pltpu.VMEM(points.shape, BF16),
        pltpu.VMEM(centres.shape, BF16), pltpu.VMEM((16, 128), I32),
        pltpu.VMEM((nz, 8, D), BF16), pltpu.VMEM((CORES, ny, nx, blk, D), BF16),
        pltpu.VMEM((8, 1024), F32), pltpu.VMEM((3, ny, 128), F32),
        pltpu.VMEM((nxc, per, 128), F32), pltpu.VMEM((nxc, per, 128), F32),
        pltpu.VMEM((nz, per, 128), F32), pltpu.VMEM((ny, per, 128), F32),
        pltpu.VMEM((nxc, per, 128), F32),
        pltpu.VMEM((nxc, 1, 128), F32), pltpu.VMEM((ny, 1, 128), F32),
        pltpu.VMEM((nz, 1, 128), F32), dma((5,)),
    ]
    scratch += [dma((15,)), dma((8,)), dma((nx * ny,)), dma((ny,))]
    cost, final = pl.pallas_call(
        functools.partial(kernel, nx, ny, nz, float(1024 * nx * ny * CORES * nz)),
        out_shape=(jax.ShapeDtypeStruct((8, 128), F32), jax.ShapeDtypeStruct((16, D), F32)),
        in_specs=[hbm] * 5,
        out_specs=(vmem, vmem),
        scratch_shapes=scratch,
        compiler_params=pltpu.CompilerParams(
            collective_id=0, has_side_effects=True, vmem_limit_bytes=60 << 20),
    )(picks, cand_assign.reshape(32, 128), assign_pts.reshape(8, 128), points, centres)
    return cost.reshape(1024), final


def solution(mesh):
    nz = mesh.shape["col"]
    nx, ny = 4, mesh.shape["row"] // (4 * CORES)
    placed = (P(("row", "col"), None), P(), P(), P(("row", "col")), P())
    return jax.shard_map(
        functools.partial(shards, nx, ny, nz),
        mesh=mesh,
        in_specs=placed,
        out_specs=(P(("row", "col")), P("row", None)),
        check_vma=False,
    )
```

```python
import functools
import jax
import jax.numpy as jnp
from jax import lax
from jax.experimental import pallas as pl
from jax.experimental.pallas import tpu as pltpu
from jax.sharding import PartitionSpec as P

K_FINAL = 1024
CORES = 2
CAP = 3
D = 256
F32, BF16, I32 = jnp.float32, jnp.bfloat16, jnp.int32
MESH = pl.DeviceIdType.MESH
BIG = 3.0e38
FAR = 1 << 20


def split3(value):
    high = value.astype(BF16)
    rest = value - high.astype(F32)
    middle = rest.astype(BF16)
    low = (rest - middle.astype(F32)).astype(BF16)
    return high, middle, low


def contract_last(left, right):
    return lax.dot_general(left, right, (((1,), (1,)), ((), ())), preferred_element_type=F32)


def near_first(size):
    return sorted(range(1, size), key=lambda step: (min(step, size - step), step))


def kernel(nx, ny, nz, npts,
           picks_hbm, owner_hbm, assign_hbm, points_hbm, centres_hbm,
           cost_ref, final_ref,
           picks_ref, owner_ref, assign_ref, pts, pts2, cen, picked, zbuf, big, nearest, meta,
           hist, hist_x, hist_z, hist_y, counts,
           tot_x, tot_y, tot_z, local_sem, ssem, rsem, block_sem, swap_sem):
    row = lax.axis_index("row")
    z = lax.axis_index("col")
    core = lax.rem(row, CORES)
    y = lax.rem(row // CORES, ny)
    x = row // (CORES * ny)
    me = row * nz + z
    slots = 2 * CAP
    rows = nz * slots
    blk = big.shape[3]
    nxc = nx * CORES

    def peer(ox=0, oy=0, oc=0, oz=0):
        px = lax.rem(x + ox, nx)
        py = lax.rem(y + oy, ny)
        pc = lax.rem(core + oc, CORES)
        return ((px * ny + py) * CORES + pc, lax.rem(z + oz, nz))

    def send(src, dst, out_sem, in_sem, device):
        pltpu.make_async_remote_copy(
            src_ref=src, dst_ref=dst, send_sem=out_sem, recv_sem=in_sem,
            device_id=device, device_id_type=MESH).start()

    def waiter(ref, sem):
        return pltpu.make_async_remote_copy(
            src_ref=ref, dst_ref=ref, send_sem=sem, recv_sem=sem,
            device_id=peer(oz=1), device_id_type=MESH)

    def arrive(ref, sem):
        waiter(ref, sem).wait_recv()

    def drain(ref, sem):
        waiter(ref, sem).wait_send()

    def others(ref, size):
        return ref.at[pl.ds(0, size - 1)]

    loads = [pltpu.make_async_copy(src, dst, local_sem.at[i]) for i, (src, dst) in enumerate(
        [(picks_hbm, picks_ref), (owner_hbm, owner_ref), (points_hbm, pts),
         (centres_hbm, cen), (assign_hbm, assign_ref)])]
    for load in loads:
        load.start()

    xc_steps = [(ox, oc) for ox in range(nx) for oc in range(CORES) if ox or oc]
    barrier = pltpu.get_barrier_semaphore()
    peers = [peer(oz=o) for o in range(1, nz)] + [peer(oy=o) for o in range(1, ny)]
    peers += [peer(ox=ox, oc=oc) for ox, oc in xc_steps]
    for other in peers:
        pl.semaphore_signal(barrier, inc=1, device_id=other, device_id_type=MESH)

    loads[0].wait()
    loads[1].wait()
    for r in range(2):
        for b in range(8):
            picked[r * 8 + b:r * 8 + b + 1, :] = picks_ref[r:r + 1, b * 128:(b + 1) * 128]
    sub = lax.broadcasted_iota(I32, (8, 128), 0)
    lane = lax.broadcasted_iota(I32, (8, 128), 1)
    local_ids, codes = [], []
    for r in range(2):
        p = picked[r * 8:(r + 1) * 8, :]
        local = p - me * 1024
        own = (local >= 0) & (local < 1024)
        local = jnp.where(own, local, FAR)
        ids = r * 1024 + sub * 128 + lane
        code = ids * 1024 + owner_ref[16 + r * 8:24 + r * 8, :] + 1
        for s in range(CAP):
            first = jnp.min(jnp.min(local, axis=1, keepdims=True), axis=0, keepdims=True)
            hit = (local == first) & (local < FAR)
            coded = jnp.where(hit, code, 0)
            codes.append(jnp.max(jnp.max(coded, axis=1, keepdims=True), axis=0, keepdims=True))
            local_ids.append(first)
            local = jnp.where(local == first, FAR, local)
    slot_row = lax.broadcasted_iota(I32, (8, 1024), 0)
    point_lane = lax.broadcasted_iota(I32, (8, 1024), 1)
    want = jnp.full((8, 1024), FAR, I32)
    for s in range(slots):
        want = jnp.where(slot_row == s, local_ids[s], want)
    choose = jnp.where(want == point_lane, 1.0, 0.0)
    choose16 = jnp.concatenate([choose, jnp.zeros((8, 1024), F32)], axis=0).astype(BF16)
    lane1 = lax.broadcasted_iota(I32, (1, 128), 1)
    lane_dev = (lane1 * 43691) >> 18
    lane_slot = lane1 - lane_dev * slots
    code_row = jnp.zeros((1, 128), I32)
    for s in range(slots):
        code_row = jnp.where(lane_slot == s, codes[s], code_row)
    digit_a = (code_row & 255).astype(F32)
    digit_b = ((code_row >> 8) & 255).astype(F32)
    digit_c = (code_row >> 16).astype(F32)
    loads[2].wait()
    loads[3].wait()
    loads[4].wait()
    mine = jnp.dot(choose16, pts[...], preferred_element_type=F32)[:8, :]
    slot_col = lax.broadcasted_iota(I32, (8, D), 0)
    filled = jnp.zeros((8, D), I32)
    for s in range(slots):
        filled = jnp.where(slot_col == s, jnp.broadcast_to(local_ids[s], (8, D)), filled)
    spare = jnp.broadcast_to(cen[0:16, :].astype(F32)[0:1, :], (8, D))
    mine = jnp.where(filled >= FAR, spare, mine)
    row_six = jnp.concatenate([digit_a, digit_b], axis=1)
    row_seven = jnp.concatenate([digit_c, digit_c], axis=1)
    mine = jnp.where(slot_col == slots, jnp.broadcast_to(row_six, (8, D)), mine)
    mine = jnp.where(slot_col == slots + 1, jnp.broadcast_to(row_seven, (8, D)), mine)
    zbuf[z] = mine.astype(BF16)

    pl.semaphore_wait(barrier, len(peers))

    for o in near_first(nz)[::-1]:
        send(zbuf.at[z], zbuf.at[z], ssem.at[0], rsem.at[0], peer(oz=o))

    acc = jnp.zeros((32, 128), F32)
    hi_iota = lax.broadcasted_iota(I32, (32, 128), 0)
    lo_iota = lax.broadcasted_iota(I32, (128, 128), 0)
    for b in range(8):
        a = assign_ref[b:b + 1, :]
        left = jnp.where(hi_iota == (a >> 7), 1.0, 0.0).astype(BF16)
        right = jnp.where(lo_iota == (a & 127), 1.0, 0.0).astype(BF16)
        acc = acc + contract_last(left, right)
    per = 32 // nxc
    for q in range(nxc):
        hist[q] = acc[q * per:(q + 1) * per, :]
    my_xc = x * CORES + core
    for ox, oc in xc_steps:
        o = ox * CORES + oc
        target = lax.rem(x + ox, nx) * CORES + lax.rem(core + oc, CORES)
        send(hist.at[target], hist_x.at[o], ssem.at[1], rsem.at[1], peer(ox=ox, oc=oc))

    p32 = pts[...].astype(F32)
    pts2[...] = (p32 * -2.0).astype(BF16)
    square = p32 * p32
    square_hi = square.astype(BF16)
    square_lo = (square - square_hi.astype(F32)).astype(BF16)
    ones = jnp.ones((16, D), BF16)
    norms = (contract_last(ones, square_hi) + contract_last(ones, square_lo))[0:1, :]

    def fold(block, masked):
        b32 = block.astype(F32)
        norm = jnp.sum(b32 * b32, axis=1, keepdims=True)
        if masked:
            place = lax.rem(lax.broadcasted_iota(I32, norm.shape, 0), blk)
            norm = jnp.where(place < rows, norm, BIG)
        for part in range(4):
            q = slice(part * 256, (part + 1) * 256)
            d = contract_last(block, pts2[q, :]) + norm
            least = jnp.min(d.reshape(d.shape[0] // 8, 8, 256), axis=0)
            nearest[:, q] = jnp.minimum(nearest[:, q], least)

    nearest[...] = jnp.full(nearest.shape, BIG, F32)

    def fold_centres(i, carry):
        fold(cen[pl.ds(pl.multiple_of(i * 512, 512), 512), :], False)
        return carry

    lax.fori_loop(0, cen.shape[0] // 512, fold_centres, 0)

    arrive(others(zbuf, nz), rsem.at[0])
    column = jnp.concatenate([zbuf[i].astype(F32) for i in range(nz)], axis=0)
    crow = lax.broadcasted_iota(I32, column.shape, 0)
    clane = lax.broadcasted_iota(I32, column.shape, 1) & 127
    cdev = (clane * 43691) >> 18
    drop = ((crow & 7) >= slots) & ((crow >> 3) != cdev)
    column = jnp.where(drop, 0.0, column).astype(BF16)
    srow = lax.broadcasted_iota(I32, (blk, nz * 8), 0)
    scol = lax.broadcasted_iota(I32, (blk, nz * 8), 1)
    sdev = (srow * 43691) >> 18
    pick = (scol == sdev * 8 + (srow - sdev * slots)) & (srow < rows)
    pick = pick | ((srow == rows) & ((scol & 7) == slots))
    pick = pick | ((srow == rows + 1) & ((scol & 7) == slots + 1))
    packed = jnp.dot(jnp.where(pick, 1.0, 0.0).astype(BF16), column, preferred_element_type=F32)
    big[0, 0, 0] = packed.astype(BF16)

    xs = near_first(nx)
    far_y = (2, ny - 2, 4)

    def slot(o, ox):
        return block_sem.at[o * nx + ox]

    def forward(o, ox, to_o, to_ox, out_sem, device):
        send(big.at[0, o, ox], big.at[0, to_o, to_ox], ssem.at[out_sem], slot(to_o, to_ox), device)

    def swap(o, ox):
        send(big.at[0, o, ox], big.at[1, o, ox], ssem.at[8], swap_sem.at[o], peer(oc=1))

    def sideways(o, ox):
        if o == 0 or o == 2:
            forward(o, ox, o + 1, ox, 11, peer(oy=1))
        if o == 0 or o == ny - 2:
            forward(o, ox, (o + ny - 1) % ny, ox, 11, peer(oy=ny - 1))

    def across(o):
        for ox in xs:
            forward(o, 0, o, ox, 10, peer(ox=ox))

    def landed(o, ox):
        arrive(big.at[0, o, ox], slot(o, ox))

    def unit(c, o):
        fold(big[c, o].reshape(nx * blk, D), True)

    def swapped(o):
        arrive(big.at[1, o], swap_sem.at[o])
        unit(1, o)

    for o in far_y:
        forward(0, 0, o, 0, 9, peer(oy=o))
    across(0)
    sideways(0, 0)
    swap(0, 0)

    arrive(others(hist_x, nxc), rsem.at[1])
    total_h = hist[my_xc]
    for o in range(1, nxc):
        total_h = total_h + hist_x[o]
    hist_z[0] = total_h
    for o in range(1, nz):
        send(hist_z.at[0], hist_z.at[o], ssem.at[2], rsem.at[2], peer(oz=o))

    for o in (1, ny - 1):
        landed(o, 0)
        swap(o, 0)
    for ox in xs:
        landed(0, ox)
        sideways(0, ox)
        swap(0, ox)
    for o in far_y:
        landed(o, 0)
        across(o)
        sideways(o, 0)
        swap(o, 0)
    unit(0, 0)

    arrive(others(hist_z, nz), rsem.at[2])
    total_h = hist_z[0]
    for o in range(1, nz):
        total_h = total_h + hist_z[o]
    hist_y[0] = total_h
    for o in range(1, ny):
        send(hist_y.at[0], hist_y.at[o], ssem.at[3], rsem.at[3], peer(oy=o))

    for o in (1, ny - 1):
        for ox in xs:
            landed(o, ox)
            swap(o, ox)
    swapped(0)
    for o in (3, ny - 3):
        landed(o, 0)
        swap(o, 0)
    unit(0, 1)
    for o in far_y[:2]:
        for ox in xs:
            landed(o, ox)
            sideways(o, ox)
            swap(o, ox)
    unit(0, ny - 1)
    for ox in xs:
        landed(4, ox)
        swap(4, ox)
    unit(0, 2)
    swapped(1)

    arrive(others(hist_y, ny), rsem.at[3])
    total_h = hist_y[0]
    for o in range(1, ny):
        total_h = total_h + hist_y[o]
    counts[my_xc] = total_h
    for ox, oc in xc_steps:
        send(counts.at[my_xc], counts.at[my_xc], ssem.at[4], rsem.at[4], peer(ox=ox, oc=oc))

    unit(0, ny - 2)
    swapped(ny - 1)
    unit(0, 4)
    for o in (3, ny - 3):
        for ox in xs:
            landed(o, ox)
            swap(o, ox)
    for o in far_y:
        swapped(o)
    for o in (3, ny - 3):
        unit(0, o)
    for o in (3, ny - 3):
        swapped(o)

    best = jnp.maximum(jnp.min(nearest[...], axis=0, keepdims=True) + norms, 0.0)
    mass = jnp.sum(best, axis=1, keepdims=True)

    def stage(buf, sem, devices, between):
        for o, device in enumerate(devices):
            send(buf.at[0], buf.at[o + 1], ssem.at[sem], rsem.at[sem], device)
        between()
        arrive(others(buf, len(devices) + 1), rsem.at[sem])
        result = buf[0]
        for o in range(len(devices)):
            result = result + buf[o + 1]
        return result

    targets = row * (K_FINAL // (nx * ny * CORES)) + lax.broadcasted_iota(I32, (16, 128), 0)
    state = {}

    def product(member, table):
        parts = jnp.concatenate(split3(member), axis=0)
        out = jnp.dot(parts, table, preferred_element_type=F32)
        return out[0:16] + out[16:32] + out[32:48]

    def lloyd_centres():
        arrive(others(counts, nxc), rsem.at[4])
        weights = 1.0 + jnp.concatenate([counts[q] for q in range(nxc)], axis=0)
        pieces = []
        for t in range(16):
            hit = jnp.broadcast_to(owner_ref[t:t + 1, :], (16, 128)) == targets
            pieces.append(jnp.where(hit, jnp.broadcast_to(weights[t:t + 1, :], (16, 128)), 0.0))
        den = pieces[0]
        for t in range(1, 16):
            den = den + pieces[t]
        state["weights"] = weights
        state["den"] = den
        state["num"] = product(jnp.concatenate(pieces, axis=1), cen[...])

    def lloyd_slots(c):
        weights = state["weights"]
        num, den = state["num"], state["den"]
        for ox in range(nx):
            for o in range(ny):
                tail = big[c, o, ox, rows - 8:rows + 8, :].astype(F32)
                meta[0, o:o + 1, :] = tail[8:9, 0:128]
                meta[1, o:o + 1, :] = tail[8:9, 128:256]
                meta[2, o:o + 1, :] = tail[9:10, 0:128]
            code = (meta[0] + meta[1] * 256.0 + meta[2] * 65536.0).astype(I32) - 1
            valid = code >= 0
            owner = jnp.where(valid, code & 1023, -1)
            ident = jnp.where(valid, code >> 10, 0)
            high = ident >> 7
            low = ident & 127
            weight = jnp.zeros((ny, 128), F32)
            for h in range(16):
                table = jnp.broadcast_to(weights[16 + h:17 + h, :], (ny, 128))
                got = jnp.take_along_axis(table, low, axis=1)
                weight = jnp.where(high == h, got, weight)
            lanes = lax.broadcasted_iota(I32, (ny, 128), 1)
            owner = jnp.where(lanes < rows, owner, -1)
            for o in range(ny):
                hit = jnp.broadcast_to(owner[o:o + 1, :], (16, 128)) == targets
                member = jnp.where(hit, jnp.broadcast_to(weight[o:o + 1, :], (16, 128)), 0.0)
                den = den + member
                num = num + product(member[:, :blk], big[c, o, ox])
        state["num"], state["den"] = num, den

    tot_x[0] = jnp.broadcast_to(mass, (1, 128))
    tot_y[0] = stage(tot_x, 5, [peer(ox=ox, oc=oc) for ox, oc in xc_steps], lloyd_centres)
    tot_z[0] = stage(tot_y, 6, [peer(oy=o) for o in range(1, ny)], lambda: lloyd_slots(0))
    total = stage(tot_z, 7, [peer(oz=o) for o in range(1, nz)], lambda: lloyd_slots(1))
    den = jnp.sum(state["den"], axis=1, keepdims=True)
    final_ref[...] = state["num"] / den
    scaled = best * npts
    for b in range(8):
        cost_ref[b:b + 1, :] = scaled[:, b * 128:(b + 1) * 128] / total
    drain(others(zbuf, nz), ssem.at[0])
    drain(others(hist_x, nxc), ssem.at[1])
    drain(others(hist_z, nz), ssem.at[2])
    drain(others(hist_y, ny), ssem.at[3])
    drain(others(counts, nxc), ssem.at[4])
    drain(others(tot_x, nxc), ssem.at[5])
    drain(others(tot_y, ny), ssem.at[6])
    drain(others(tot_z, nz), ssem.at[7])
    drain(big.at[1], ssem.at[8])
    drain(big.at[0, 0, pl.ds(0, 3)], ssem.at[9])
    drain(big.at[0, pl.ds(0, nx - 1)], ssem.at[10])
    drain(big.at[0, pl.ds(0, 4)], ssem.at[11])


def shards(nx, ny, nz, points, centres, picks, assign_pts, cand_assign):
    nxc = nx * CORES
    blk = (nz * 2 * CAP + 2 + 15) // 16 * 16
    dma = pltpu.SemaphoreType.DMA
    per = 32 // nxc
    vmem = pl.BlockSpec(memory_space=pltpu.VMEM)
    hbm = pl.BlockSpec(memory_space=pltpu.MemorySpace.HBM)
    scratch = [
        pltpu.VMEM(picks.shape, I32), pltpu.VMEM((32, 128), I32), pltpu.VMEM((8, 128), I32),
        pltpu.VMEM(points.shape, BF16), pltpu.VMEM(points.shape, BF16),
        pltpu.VMEM(centres.shape, BF16), pltpu.VMEM((16, 128), I32),
        pltpu.VMEM((nz, 8, D), BF16), pltpu.VMEM((CORES, ny, nx, blk, D), BF16),
        pltpu.VMEM((8, 1024), F32), pltpu.VMEM((3, ny, 128), F32),
        pltpu.VMEM((nxc, per, 128), F32), pltpu.VMEM((nxc, per, 128), F32),
        pltpu.VMEM((nz, per, 128), F32), pltpu.VMEM((ny, per, 128), F32),
        pltpu.VMEM((nxc, per, 128), F32),
        pltpu.VMEM((nxc, 1, 128), F32), pltpu.VMEM((ny, 1, 128), F32),
        pltpu.VMEM((nz, 1, 128), F32), dma((5,)),
    ]
    scratch += [dma((12,)), dma((8,)), dma((nx * ny,)), dma((ny,))]
    cost, final = pl.pallas_call(
        functools.partial(kernel, nx, ny, nz, float(1024 * nx * ny * CORES * nz)),
        out_shape=(jax.ShapeDtypeStruct((8, 128), F32), jax.ShapeDtypeStruct((16, D), F32)),
        in_specs=[hbm] * 5,
        out_specs=(vmem, vmem),
        scratch_shapes=scratch,
        compiler_params=pltpu.CompilerParams(
            collective_id=0, has_side_effects=True, vmem_limit_bytes=60 << 20),
    )(picks, cand_assign.reshape(32, 128), assign_pts.reshape(8, 128), points, centres)
    return cost.reshape(1024), final


def solution(mesh):
    nz = mesh.shape["col"]
    nx, ny = 4, mesh.shape["row"] // (4 * CORES)
    placed = (P(("row", "col"), None), P(), P(), P(("row", "col")), P())
    return jax.shard_map(
        functools.partial(shards, nx, ny, nz),
        mesh=mesh,
        in_specs=placed,
        out_specs=(P(("row", "col")), P("row", None)),
        check_vma=False,
    )
```

```python
import functools
import jax
import jax.numpy as jnp
from jax import lax
from jax.experimental import pallas as pl
from jax.experimental.pallas import tpu as pltpu
from jax.sharding import PartitionSpec as P

K_FINAL = 1024
CORES = 2
CAP = 3
D = 256
F32, BF16, I32 = jnp.float32, jnp.bfloat16, jnp.int32
MESH = pl.DeviceIdType.MESH
BIG = 3.0e38
FAR = 1 << 20


def split3(value):
    high = value.astype(BF16)
    rest = value - high.astype(F32)
    middle = rest.astype(BF16)
    low = (rest - middle.astype(F32)).astype(BF16)
    return high, middle, low


def contract_last(left, right):
    return lax.dot_general(left, right, (((1,), (1,)), ((), ())), preferred_element_type=F32)


def near_first(size):
    return sorted(range(1, size), key=lambda step: (min(step, size - step), step))


def kernel(nx, ny, nz, npts,
           picks_hbm, owner_hbm, assign_hbm, points_hbm, centres_hbm,
           cost_ref, final_ref,
           picks_ref, owner_ref, assign_ref, pts, pts2, cen, picked, zbuf, big, nearest, meta,
           hist, hist_x, hist_z, hist_y, counts,
           tot_p, tot_z, local_sem, ssem, rsem, block_sem, swap_sem):
    row = lax.axis_index("row")
    z = lax.axis_index("col")
    core = lax.rem(row, CORES)
    y = lax.rem(row // CORES, ny)
    x = row // (CORES * ny)
    me = row * nz + z
    slots = 2 * CAP
    rows = nz * slots
    blk = big.shape[3]
    nxc = nx * CORES

    def peer(ox=0, oy=0, oc=0, oz=0):
        px = lax.rem(x + ox, nx)
        py = lax.rem(y + oy, ny)
        pc = lax.rem(core + oc, CORES)
        return ((px * ny + py) * CORES + pc, lax.rem(z + oz, nz))

    def send(src, dst, out_sem, in_sem, device):
        pltpu.make_async_remote_copy(
            src_ref=src, dst_ref=dst, send_sem=out_sem, recv_sem=in_sem,
            device_id=device, device_id_type=MESH).start()

    def waiter(ref, sem):
        return pltpu.make_async_remote_copy(
            src_ref=ref, dst_ref=ref, send_sem=sem, recv_sem=sem,
            device_id=peer(oz=1), device_id_type=MESH)

    def arrive(ref, sem):
        waiter(ref, sem).wait_recv()

    def drain(ref, sem):
        waiter(ref, sem).wait_send()

    def others(ref, size):
        return ref.at[pl.ds(0, size - 1)]

    loads = [pltpu.make_async_copy(src, dst, local_sem.at[i]) for i, (src, dst) in enumerate(
        [(picks_hbm, picks_ref), (owner_hbm, owner_ref), (points_hbm, pts),
         (centres_hbm, cen), (assign_hbm, assign_ref)])]
    for load in loads:
        load.start()

    xc_steps = [(ox, oc) for ox in range(nx) for oc in range(CORES) if ox or oc]
    barrier = pltpu.get_barrier_semaphore()
    plane = [(ox, oy, oc) for ox in range(nx) for oy in range(ny) for oc in range(CORES)][1:]
    plane.sort(key=lambda p: -min(p[0], nx - p[0]) - min(p[1], ny - p[1]))
    plane_peers = [peer(ox=ox, oy=oy, oc=oc) for ox, oy, oc in plane]
    peers = [peer(oz=o) for o in range(1, nz)] + plane_peers
    for other in peers:
        pl.semaphore_signal(barrier, inc=1, device_id=other, device_id_type=MESH)

    loads[0].wait()
    loads[1].wait()
    for r in range(2):
        for b in range(8):
            picked[r * 8 + b:r * 8 + b + 1, :] = picks_ref[r:r + 1, b * 128:(b + 1) * 128]
    sub = lax.broadcasted_iota(I32, (8, 128), 0)
    lane = lax.broadcasted_iota(I32, (8, 128), 1)
    local_ids, codes = [], []
    for r in range(2):
        p = picked[r * 8:(r + 1) * 8, :]
        local = p - me * 1024
        own = (local >= 0) & (local < 1024)
        local = jnp.where(own, local, FAR)
        ids = r * 1024 + sub * 128 + lane
        code = ids * 1024 + owner_ref[16 + r * 8:24 + r * 8, :] + 1
        for s in range(CAP):
            first = jnp.min(jnp.min(local, axis=1, keepdims=True), axis=0, keepdims=True)
            hit = (local == first) & (local < FAR)
            coded = jnp.where(hit, code, 0)
            codes.append(jnp.max(jnp.max(coded, axis=1, keepdims=True), axis=0, keepdims=True))
            local_ids.append(first)
            local = jnp.where(local == first, FAR, local)
    slot_row = lax.broadcasted_iota(I32, (8, 1024), 0)
    point_lane = lax.broadcasted_iota(I32, (8, 1024), 1)
    want = jnp.full((8, 1024), FAR, I32)
    for s in range(slots):
        want = jnp.where(slot_row == s, local_ids[s], want)
    choose = jnp.where(want == point_lane, 1.0, 0.0)
    choose16 = jnp.concatenate([choose, jnp.zeros((8, 1024), F32)], axis=0).astype(BF16)
    lane1 = lax.broadcasted_iota(I32, (1, 128), 1)
    lane_dev = (lane1 * 43691) >> 18
    lane_slot = lane1 - lane_dev * slots
    code_row = jnp.zeros((1, 128), I32)
    for s in range(slots):
        code_row = jnp.where(lane_slot == s, codes[s], code_row)
    digit_a = (code_row & 255).astype(F32)
    digit_b = ((code_row >> 8) & 255).astype(F32)
    digit_c = (code_row >> 16).astype(F32)
    loads[2].wait()
    loads[3].wait()
    loads[4].wait()
    mine = jnp.dot(choose16, pts[...], preferred_element_type=F32)[:8, :]
    slot_col = lax.broadcasted_iota(I32, (8, D), 0)
    filled = jnp.zeros((8, D), I32)
    for s in range(slots):
        filled = jnp.where(slot_col == s, jnp.broadcast_to(local_ids[s], (8, D)), filled)
    spare = jnp.broadcast_to(cen[0:16, :].astype(F32)[0:1, :], (8, D))
    mine = jnp.where(filled >= FAR, spare, mine)
    row_six = jnp.concatenate([digit_a, digit_b], axis=1)
    row_seven = jnp.concatenate([digit_c, digit_c], axis=1)
    mine = jnp.where(slot_col == slots, jnp.broadcast_to(row_six, (8, D)), mine)
    mine = jnp.where(slot_col == slots + 1, jnp.broadcast_to(row_seven, (8, D)), mine)
    zbuf[z] = mine.astype(BF16)

    pl.semaphore_wait(barrier, len(peers))

    for o in near_first(nz)[::-1]:
        send(zbuf.at[z], zbuf.at[z], ssem.at[0], rsem.at[0], peer(oz=o))

    acc = jnp.zeros((32, 128), F32)
    hi_iota = lax.broadcasted_iota(I32, (32, 128), 0)
    lo_iota = lax.broadcasted_iota(I32, (128, 128), 0)
    for b in range(8):
        a = assign_ref[b:b + 1, :]
        left = jnp.where(hi_iota == (a >> 7), 1.0, 0.0).astype(BF16)
        right = jnp.where(lo_iota == (a & 127), 1.0, 0.0).astype(BF16)
        acc = acc + contract_last(left, right)
    per = 32 // nxc
    for q in range(nxc):
        hist[q] = acc[q * per:(q + 1) * per, :]
    my_xc = x * CORES + core
    for ox, oc in xc_steps:
        o = ox * CORES + oc
        target = lax.rem(x + ox, nx) * CORES + lax.rem(core + oc, CORES)
        send(hist.at[target], hist_x.at[o], ssem.at[1], rsem.at[1], peer(ox=ox, oc=oc))

    p32 = pts[...].astype(F32)
    pts2[...] = (p32 * -2.0).astype(BF16)
    square = p32 * p32
    square_hi = square.astype(BF16)
    square_lo = (square - square_hi.astype(F32)).astype(BF16)
    ones = jnp.ones((16, D), BF16)
    norms = (contract_last(ones, square_hi) + contract_last(ones, square_lo))[0:1, :]

    def fold(block, masked):
        b32 = block.astype(F32)
        norm = jnp.sum(b32 * b32, axis=1, keepdims=True)
        if masked:
            place = lax.rem(lax.broadcasted_iota(I32, norm.shape, 0), blk)
            norm = jnp.where(place < rows, norm, BIG)
        for part in range(4):
            q = slice(part * 256, (part + 1) * 256)
            d = contract_last(block, pts2[q, :]) + norm
            least = jnp.min(d.reshape(d.shape[0] // 8, 8, 256), axis=0)
            nearest[:, q] = jnp.minimum(nearest[:, q], least)

    nearest[...] = jnp.full(nearest.shape, BIG, F32)

    def fold_centres(i, carry):
        fold(cen[pl.ds(pl.multiple_of(i * 512, 512), 512), :], False)
        return carry

    lax.fori_loop(0, cen.shape[0] // 512, fold_centres, 0)

    arrive(others(zbuf, nz), rsem.at[0])
    column = jnp.concatenate([zbuf[i].astype(F32) for i in range(nz)], axis=0)
    crow = lax.broadcasted_iota(I32, column.shape, 0)
    clane = lax.broadcasted_iota(I32, column.shape, 1) & 127
    cdev = (clane * 43691) >> 18
    drop = ((crow & 7) >= slots) & ((crow >> 3) != cdev)
    column = jnp.where(drop, 0.0, column).astype(BF16)
    srow = lax.broadcasted_iota(I32, (blk, nz * 8), 0)
    scol = lax.broadcasted_iota(I32, (blk, nz * 8), 1)
    sdev = (srow * 43691) >> 18
    pick = (scol == sdev * 8 + (srow - sdev * slots)) & (srow < rows)
    pick = pick | ((srow == rows) & ((scol & 7) == slots))
    pick = pick | ((srow == rows + 1) & ((scol & 7) == slots + 1))
    packed = jnp.dot(jnp.where(pick, 1.0, 0.0).astype(BF16), column, preferred_element_type=F32)
    big[0, 0, 0] = packed.astype(BF16)

    xs = near_first(nx)
    near_x = (1, nx - 1)
    far_y = (2, ny - 2, 4)

    def slot(o, ox):
        return block_sem.at[o * nx + ox]

    def forward(o, ox, to_o, to_ox, out_sem, device):
        send(big.at[0, o, ox], big.at[0, to_o, to_ox], ssem.at[out_sem], slot(to_o, to_ox), device)

    def swap(o, ox):
        send(big.at[0, o, ox], big.at[1, o, ox], ssem.at[8], swap_sem.at[o], peer(oc=1))

    def sideways(o, ox):
        if o == 0 and ox in near_x:
            return
        if o == 0 or o == 2:
            forward(o, ox, o + 1, ox, 11, peer(oy=1))
        if o == 0 or o == ny - 2:
            forward(o, ox, (o + ny - 1) % ny, ox, 11, peer(oy=ny - 1))

    def across(o):
        for ox in xs:
            forward(o, 0, o, ox, 10, peer(ox=ox))

    def landed(o, ox):
        arrive(big.at[0, o, ox], slot(o, ox))

    def unit(c, o):
        fold(big[c, o].reshape(nx * blk, D), True)

    def swapped(o):
        arrive(big.at[1, o], swap_sem.at[o])
        unit(1, o)

    for o in far_y:
        forward(0, 0, o, 0, 9, peer(oy=o))
    across(0)
    sideways(0, 0)
    swap(0, 0)

    arrive(others(hist_x, nxc), rsem.at[1])
    total_h = hist[my_xc]
    for o in range(1, nxc):
        total_h = total_h + hist_x[o]
    hist_z[0] = total_h
    for o in range(1, nz):
        send(hist_z.at[0], hist_z.at[o], ssem.at[2], rsem.at[2], peer(oz=o))

    for o in (1, ny - 1):
        landed(o, 0)
        for ox in near_x:
            forward(o, 0, o, ox, 10, peer(ox=ox))
        swap(o, 0)
    for ox in xs:
        landed(0, ox)
        sideways(0, ox)
        swap(0, ox)
    for o in far_y:
        landed(o, 0)
        across(o)
        sideways(o, 0)
        swap(o, 0)
    unit(0, 0)

    arrive(others(hist_z, nz), rsem.at[2])
    total_h = hist_z[0]
    for o in range(1, nz):
        total_h = total_h + hist_z[o]
    hist_y[0] = total_h
    for o in range(1, ny):
        send(hist_y.at[0], hist_y.at[o], ssem.at[3], rsem.at[3], peer(oy=o))

    for o in (1, ny - 1):
        for ox in xs:
            landed(o, ox)
            swap(o, ox)
    swapped(0)
    for o in (3, ny - 3):
        landed(o, 0)
        swap(o, 0)
    unit(0, 1)
    for o in far_y[:2]:
        for ox in xs:
            landed(o, ox)
            sideways(o, ox)
            swap(o, ox)
    unit(0, ny - 1)
    for ox in xs:
        landed(4, ox)
        swap(4, ox)
    unit(0, 2)
    swapped(1)

    arrive(others(hist_y, ny), rsem.at[3])
    total_h = hist_y[0]
    for o in range(1, ny):
        total_h = total_h + hist_y[o]
    counts[my_xc] = total_h
    for ox, oc in xc_steps:
        send(counts.at[my_xc], counts.at[my_xc], ssem.at[4], rsem.at[4], peer(ox=ox, oc=oc))

    unit(0, ny - 2)
    swapped(ny - 1)
    unit(0, 4)
    for o in (3, ny - 3):
        for ox in xs:
            landed(o, ox)
            swap(o, ox)
    for o in far_y:
        swapped(o)
    for o in (3, ny - 3):
        unit(0, o)
    for o in (3, ny - 3):
        swapped(o)

    best = jnp.maximum(jnp.min(nearest[...], axis=0, keepdims=True) + norms, 0.0)
    mass = jnp.sum(best, axis=1, keepdims=True)

    def stage(buf, sem, devices, between):
        for o, device in enumerate(devices):
            send(buf.at[0], buf.at[o + 1], ssem.at[sem], rsem.at[sem], device)
        between()
        arrive(others(buf, len(devices) + 1), rsem.at[sem])
        return jnp.sum(buf[...], axis=0)

    targets = row * (K_FINAL // (nx * ny * CORES)) + lax.broadcasted_iota(I32, (16, 128), 0)
    state = {}

    def product(member, table):
        parts = jnp.concatenate(split3(member), axis=0)
        out = jnp.dot(parts, table, preferred_element_type=F32)
        return out[0:16] + out[16:32] + out[32:48]

    def lloyd_centres():
        arrive(others(counts, nxc), rsem.at[4])
        weights = 1.0 + jnp.concatenate([counts[q] for q in range(nxc)], axis=0)
        pieces = []
        for t in range(16):
            hit = jnp.broadcast_to(owner_ref[t:t + 1, :], (16, 128)) == targets
            pieces.append(jnp.where(hit, jnp.broadcast_to(weights[t:t + 1, :], (16, 128)), 0.0))
        den = pieces[0]
        for t in range(1, 16):
            den = den + pieces[t]
        state["weights"] = weights
        state["den"] = den
        state["num"] = product(jnp.concatenate(pieces, axis=1), cen[...])

    def lloyd_slots(c):
        weights = state["weights"]
        num, den = state["num"], state["den"]
        for ox in range(nx):
            for o in range(ny):
                tail = big[c, o, ox, rows - 8:rows + 8, :].astype(F32)
                meta[0, o:o + 1, :] = tail[8:9, 0:128]
                meta[1, o:o + 1, :] = tail[8:9, 128:256]
                meta[2, o:o + 1, :] = tail[9:10, 0:128]
            code = (meta[0] + meta[1] * 256.0 + meta[2] * 65536.0).astype(I32) - 1
            valid = code >= 0
            owner = jnp.where(valid, code & 1023, -1)
            ident = jnp.where(valid, code >> 10, 0)
            high = ident >> 7
            low = ident & 127
            weight = jnp.zeros((ny, 128), F32)
            for h in range(16):
                table = jnp.broadcast_to(weights[16 + h:17 + h, :], (ny, 128))
                got = jnp.take_along_axis(table, low, axis=1)
                weight = jnp.where(high == h, got, weight)
            lanes = lax.broadcasted_iota(I32, (ny, 128), 1)
            owner = jnp.where(lanes < rows, owner, -1)
            for o in range(ny):
                hit = jnp.broadcast_to(owner[o:o + 1, :], (16, 128)) == targets
                member = jnp.where(hit, jnp.broadcast_to(weight[o:o + 1, :], (16, 128)), 0.0)
                den = den + member
                num = num + product(member[:, :blk], big[c, o, ox])
        state["num"], state["den"] = num, den

    def lloyd_first():
        lloyd_centres()
        lloyd_slots(0)

    tot_p[0] = jnp.broadcast_to(mass, (1, 128))
    tot_z[0] = stage(tot_p, 5, plane_peers, lloyd_first)
    total = stage(tot_z, 7, [peer(oz=o) for o in range(1, nz)], lambda: lloyd_slots(1))
    den = jnp.sum(state["den"], axis=1, keepdims=True)
    final_ref[...] = state["num"] / den
    scaled = best * npts
    for b in range(8):
        cost_ref[b:b + 1, :] = scaled[:, b * 128:(b + 1) * 128] / total
    drain(others(zbuf, nz), ssem.at[0])
    drain(others(hist_x, nxc), ssem.at[1])
    drain(others(hist_z, nz), ssem.at[2])
    drain(others(hist_y, ny), ssem.at[3])
    drain(others(counts, nxc), ssem.at[4])
    drain(others(tot_p, nxc * ny), ssem.at[5])
    drain(others(tot_z, nz), ssem.at[7])
    drain(big.at[1], ssem.at[8])
    drain(big.at[0, 0, pl.ds(0, 3)], ssem.at[9])
    drain(big.at[0, pl.ds(0, 4)], ssem.at[10])
    drain(big.at[0, pl.ds(0, 3)], ssem.at[11])


def hand_over(cost_ref, final_ref, cost_out, final_out):
    cost_out[...] = cost_ref[...]
    final_out[...] = final_ref[...]


def shards(nx, ny, nz, points, centres, picks, assign_pts, cand_assign):
    nxc = nx * CORES
    blk = (nz * 2 * CAP + 2 + 15) // 16 * 16
    dma = pltpu.SemaphoreType.DMA
    per = 32 // nxc
    vmem = pl.BlockSpec(memory_space=pltpu.VMEM)
    hbm = pl.BlockSpec(memory_space=pltpu.MemorySpace.HBM)
    scratch = [
        pltpu.VMEM(picks.shape, I32), pltpu.VMEM((32, 128), I32), pltpu.VMEM((8, 128), I32),
        pltpu.VMEM(points.shape, BF16), pltpu.VMEM(points.shape, BF16),
        pltpu.VMEM(centres.shape, BF16), pltpu.VMEM((16, 128), I32),
        pltpu.VMEM((nz, 8, D), BF16), pltpu.VMEM((CORES, ny, nx, blk, D), BF16),
        pltpu.VMEM((8, 1024), F32), pltpu.VMEM((3, ny, 128), F32),
        pltpu.VMEM((nxc, per, 128), F32), pltpu.VMEM((nxc, per, 128), F32),
        pltpu.VMEM((nz, per, 128), F32), pltpu.VMEM((ny, per, 128), F32),
        pltpu.VMEM((nxc, per, 128), F32),
        pltpu.VMEM((nxc * ny, 1, 128), F32), pltpu.VMEM((nz, 1, 128), F32), dma((5,)),
    ]
    scratch += [dma((12,)), dma((8,)), dma((nx * ny,)), dma((ny,))]
    cost, final = pl.pallas_call(
        functools.partial(kernel, nx, ny, nz, float(1024 * nx * ny * CORES * nz)),
        out_shape=(jax.ShapeDtypeStruct((8, 128), F32), jax.ShapeDtypeStruct((16, D), F32)),
        in_specs=[hbm] * 5,
        out_specs=(vmem, vmem),
        scratch_shapes=scratch,
        compiler_params=pltpu.CompilerParams(
            collective_id=0, has_side_effects=True, vmem_limit_bytes=60 << 20),
    )(picks, cand_assign.reshape(32, 128), assign_pts.reshape(8, 128), points, centres)
    cost, final = pl.pallas_call(
        hand_over,
        out_shape=(jax.ShapeDtypeStruct((8, 128), F32), jax.ShapeDtypeStruct((16, D), F32)),
    )(cost, final)
    return cost.reshape(1024), final


def solution(mesh):
    nz = mesh.shape["col"]
    nx, ny = 4, mesh.shape["row"] // (4 * CORES)
    placed = (P(("row", "col"), None), P(), P(), P(("row", "col")), P())
    return jax.shard_map(
        functools.partial(shards, nx, ny, nz),
        mesh=mesh,
        in_specs=placed,
        out_specs=(P(("row", "col")), P("row", None)),
        check_vma=False,
    )
```

```python
import functools
import jax
import jax.numpy as jnp
from jax import lax
from jax.experimental import pallas as pl
from jax.experimental.pallas import tpu as pltpu
from jax.sharding import PartitionSpec as P

K_FINAL = 1024
CORES = 2
CAP = 3
D = 256
F32, BF16, I32 = jnp.float32, jnp.bfloat16, jnp.int32
MESH = pl.DeviceIdType.MESH
BIG = 3.0e38
FAR = 1 << 20


def split3(value):
    high = value.astype(BF16)
    rest = value - high.astype(F32)
    middle = rest.astype(BF16)
    low = (rest - middle.astype(F32)).astype(BF16)
    return high, middle, low


def contract_last(left, right):
    return lax.dot_general(left, right, (((1,), (1,)), ((), ())), preferred_element_type=F32)


def near_first(size):
    return sorted(range(1, size), key=lambda step: (min(step, size - step), step))


def kernel(nx, ny, nz, npts,
           picks_hbm, owner_hbm, assign_hbm, points_hbm, centres_hbm,
           cost_ref, final_ref,
           picks_ref, owner_ref, assign_ref, first_rows, pts, pts2, cen, picked, zbuf, big, nearest, meta,
           hist, hist_x, hist_z, hist_y, counts,
           tot_p, tot_z, local_sem, ssem, rsem, block_sem, swap_sem):
    row = lax.axis_index("row")
    z = lax.axis_index("col")
    core = lax.rem(row, CORES)
    y = lax.rem(row // CORES, ny)
    x = row // (CORES * ny)
    me = row * nz + z
    slots = 2 * CAP
    rows = nz * slots
    blk = big.shape[3]
    nxc = nx * CORES

    def peer(ox=0, oy=0, oc=0, oz=0):
        px = lax.rem(x + ox, nx)
        py = lax.rem(y + oy, ny)
        pc = lax.rem(core + oc, CORES)
        return ((px * ny + py) * CORES + pc, lax.rem(z + oz, nz))

    def send(src, dst, out_sem, in_sem, device):
        pltpu.make_async_remote_copy(
            src_ref=src, dst_ref=dst, send_sem=out_sem, recv_sem=in_sem,
            device_id=device, device_id_type=MESH).start()

    def waiter(ref, sem):
        return pltpu.make_async_remote_copy(
            src_ref=ref, dst_ref=ref, send_sem=sem, recv_sem=sem,
            device_id=peer(oz=1), device_id_type=MESH)

    def arrive(ref, sem):
        waiter(ref, sem).wait_recv()

    def drain(ref, sem):
        waiter(ref, sem).wait_send()

    def others(ref, size):
        return ref.at[pl.ds(0, size - 1)]

    loads = [pltpu.make_async_copy(src, dst, local_sem.at[i]) for i, (src, dst) in enumerate(
        [(picks_hbm, picks_ref), (owner_hbm, owner_ref), (points_hbm, pts),
         (centres_hbm.at[pl.ds(0, 16)], first_rows), (centres_hbm, cen), (assign_hbm, assign_ref)])]
    for load in loads:
        load.start()

    xc_steps = [(ox, oc) for ox in range(nx) for oc in range(CORES) if ox or oc]
    barrier = pltpu.get_barrier_semaphore()
    plane = [(ox, oy, oc) for ox in range(nx) for oy in range(ny) for oc in range(CORES)][1:]
    plane.sort(key=lambda p: -min(p[0], nx - p[0]) - min(p[1], ny - p[1]))
    plane_peers = [peer(ox=ox, oy=oy, oc=oc) for ox, oy, oc in plane]
    peers = [peer(oz=o) for o in near_first(nz)[::-1]] + plane_peers
    for other in peers:
        pl.semaphore_signal(barrier, inc=1, device_id=other, device_id_type=MESH)

    loads[0].wait()
    loads[1].wait()
    for r in range(2):
        for b in range(8):
            picked[r * 8 + b:r * 8 + b + 1, :] = picks_ref[r:r + 1, b * 128:(b + 1) * 128]
    sub = lax.broadcasted_iota(I32, (8, 128), 0)
    lane = lax.broadcasted_iota(I32, (8, 128), 1)
    local_ids, codes = [], []
    for r in range(2):
        p = picked[r * 8:(r + 1) * 8, :]
        local = p - me * 1024
        own = (local >= 0) & (local < 1024)
        local = jnp.where(own, local, FAR)
        ids = r * 1024 + sub * 128 + lane
        code = ids * 1024 + owner_ref[16 + r * 8:24 + r * 8, :] + 1
        for s in range(CAP):
            first = jnp.min(jnp.min(local, axis=1, keepdims=True), axis=0, keepdims=True)
            hit = (local == first) & (local < FAR)
            coded = jnp.where(hit, code, 0)
            codes.append(jnp.max(jnp.max(coded, axis=1, keepdims=True), axis=0, keepdims=True))
            local_ids.append(first)
            local = jnp.where(local == first, FAR, local)
    slot_row = lax.broadcasted_iota(I32, (8, 1024), 0)
    point_lane = lax.broadcasted_iota(I32, (8, 1024), 1)
    want = jnp.full((8, 1024), FAR, I32)
    for s in range(slots):
        want = jnp.where(slot_row == s, local_ids[s], want)
    choose = jnp.where(want == point_lane, 1.0, 0.0)
    choose16 = jnp.concatenate([choose, jnp.zeros((8, 1024), F32)], axis=0).astype(BF16)
    lane1 = lax.broadcasted_iota(I32, (1, 128), 1)
    lane_dev = (lane1 * 43691) >> 18
    lane_slot = lane1 - lane_dev * slots
    code_row = jnp.zeros((1, 128), I32)
    for s in range(slots):
        code_row = jnp.where(lane_slot == s, codes[s], code_row)
    digit_a = (code_row & 255).astype(F32)
    digit_b = ((code_row >> 8) & 255).astype(F32)
    digit_c = (code_row >> 16).astype(F32)
    loads[2].wait()
    loads[3].wait()
    mine = jnp.dot(choose16, pts[...], preferred_element_type=F32)[:8, :]
    slot_col = lax.broadcasted_iota(I32, (8, D), 0)
    filled = jnp.zeros((8, D), I32)
    for s in range(slots):
        filled = jnp.where(slot_col == s, jnp.broadcast_to(local_ids[s], (8, D)), filled)
    spare = jnp.broadcast_to(first_rows[...].astype(F32)[0:1, :], (8, D))
    mine = jnp.where(filled >= FAR, spare, mine)
    row_six = jnp.concatenate([digit_a, digit_b], axis=1)
    row_seven = jnp.concatenate([digit_c, digit_c], axis=1)
    mine = jnp.where(slot_col == slots, jnp.broadcast_to(row_six, (8, D)), mine)
    mine = jnp.where(slot_col == slots + 1, jnp.broadcast_to(row_seven, (8, D)), mine)
    zbuf[z] = mine.astype(BF16)

    pl.semaphore_wait(barrier, len(peers))

    for o in near_first(nz)[::-1]:
        send(zbuf.at[z], zbuf.at[z], ssem.at[0], rsem.at[0], peer(oz=o))

    loads[4].wait()
    loads[5].wait()
    acc = jnp.zeros((32, 128), F32)
    hi_iota = lax.broadcasted_iota(I32, (32, 128), 0)
    lo_iota = lax.broadcasted_iota(I32, (128, 128), 0)
    for b in range(8):
        a = assign_ref[b:b + 1, :]
        left = jnp.where(hi_iota == (a >> 7), 1.0, 0.0).astype(BF16)
        right = jnp.where(lo_iota == (a & 127), 1.0, 0.0).astype(BF16)
        acc = acc + contract_last(left, right)
    per = 32 // nxc
    for q in range(nxc):
        hist[q] = acc[q * per:(q + 1) * per, :]
    my_xc = x * CORES + core
    for ox, oc in xc_steps:
        o = ox * CORES + oc
        target = lax.rem(x + ox, nx) * CORES + lax.rem(core + oc, CORES)
        send(hist.at[target], hist_x.at[o], ssem.at[1], rsem.at[1], peer(ox=ox, oc=oc))

    p32 = pts[...].astype(F32)
    pts2[...] = (p32 * -2.0).astype(BF16)
    square = p32 * p32
    square_hi = square.astype(BF16)
    square_lo = (square - square_hi.astype(F32)).astype(BF16)
    ones = jnp.ones((16, D), BF16)
    norms = (contract_last(ones, square_hi) + contract_last(ones, square_lo))[0:1, :]

    def fold(block, masked):
        b32 = block.astype(F32)
        norm = jnp.sum(b32 * b32, axis=1, keepdims=True)
        if masked:
            place = lax.rem(lax.broadcasted_iota(I32, norm.shape, 0), blk)
            norm = jnp.where(place < rows, norm, BIG)
        for part in range(4):
            q = slice(part * 256, (part + 1) * 256)
            d = contract_last(block, pts2[q, :]) + norm
            least = jnp.min(d.reshape(d.shape[0] // 8, 8, 256), axis=0)
            nearest[:, q] = jnp.minimum(nearest[:, q], least)

    nearest[...] = jnp.full(nearest.shape, BIG, F32)

    def fold_centres(i, carry):
        fold(cen[pl.ds(pl.multiple_of(i * 512, 512), 512), :], False)
        return carry

    lax.fori_loop(0, cen.shape[0] // 512, fold_centres, 0)

    srow = lax.broadcasted_iota(I32, (blk, nz * 8), 0)
    scol = lax.broadcasted_iota(I32, (blk, nz * 8), 1)
    sdev = (srow * 43691) >> 18
    pick = (scol == sdev * 8 + (srow - sdev * slots)) & (srow < rows)
    pick = pick | ((srow == rows) & ((scol & 7) == slots))
    pick = pick | ((srow == rows + 1) & ((scol & 7) == slots + 1))
    choose_rows = jnp.where(pick, 1.0, 0.0).astype(BF16)
    arrive(others(zbuf, nz), rsem.at[0])
    column = jnp.concatenate([zbuf[i].astype(F32) for i in range(nz)], axis=0)
    crow = lax.broadcasted_iota(I32, column.shape, 0)
    clane = lax.broadcasted_iota(I32, column.shape, 1) & 127
    cdev = (clane * 43691) >> 18
    drop = ((crow & 7) >= slots) & ((crow >> 3) != cdev)
    column = jnp.where(drop, 0.0, column).astype(BF16)
    packed = jnp.dot(choose_rows, column, preferred_element_type=F32)
    big[0, 0, 0] = packed.astype(BF16)

    xs = near_first(nx)
    far_y = (2, ny - 2, 4)

    def slot(o, ox):
        return block_sem.at[o * nx + ox]

    def forward(o, ox, to_o, to_ox, out_sem, device):
        send(big.at[0, o, ox], big.at[0, to_o, to_ox], ssem.at[out_sem], slot(to_o, to_ox), device)

    def swap(o, ox):
        send(big.at[0, o, ox], big.at[1, o, ox], ssem.at[8], swap_sem.at[o], peer(oc=1))

    def sideways(o, ox):
        if o == 0 or o == 2:
            forward(o, ox, o + 1, ox, 11, peer(oy=1))
        if o == 0 or o == ny - 2:
            forward(o, ox, (o + ny - 1) % ny, ox, 11, peer(oy=ny - 1))

    def across(o):
        for ox in xs:
            forward(o, 0, o, ox, 10, peer(ox=ox))

    def landed(o, ox):
        arrive(big.at[0, o, ox], slot(o, ox))

    def unit(c, o):
        fold(big[c, o].reshape(nx * blk, D), True)

    def swapped(o):
        arrive(big.at[1, o], swap_sem.at[o])
        unit(1, o)

    for o in far_y:
        forward(0, 0, o, 0, 9, peer(oy=o))
    across(0)
    sideways(0, 0)
    swap(0, 0)

    arrive(others(hist_x, nxc), rsem.at[1])
    total_h = hist[my_xc]
    for o in range(1, nxc):
        total_h = total_h + hist_x[o]
    hist_z[0] = total_h
    for o in range(1, nz):
        send(hist_z.at[0], hist_z.at[o], ssem.at[2], rsem.at[2], peer(oz=o))

    for o in (1, ny - 1):
        landed(o, 0)
        swap(o, 0)
    for ox in xs:
        landed(0, ox)
        sideways(0, ox)
        swap(0, ox)
    for o in far_y:
        landed(o, 0)
        across(o)
        sideways(o, 0)
        swap(o, 0)
    unit(0, 0)

    arrive(others(hist_z, nz), rsem.at[2])
    total_h = hist_z[0]
    for o in range(1, nz):
        total_h = total_h + hist_z[o]
    hist_y[0] = total_h
    for o in range(1, ny):
        send(hist_y.at[0], hist_y.at[o], ssem.at[3], rsem.at[3], peer(oy=o))

    for o in (1, ny - 1):
        for ox in xs:
            landed(o, ox)
            swap(o, ox)
    swapped(0)
    for o in (3, ny - 3):
        landed(o, 0)
        swap(o, 0)
    unit(0, 1)
    for o in far_y[:2]:
        for ox in xs:
            landed(o, ox)
            sideways(o, ox)
            swap(o, ox)
    unit(0, ny - 1)
    for ox in xs:
        landed(4, ox)
        swap(4, ox)
    unit(0, 2)
    swapped(1)

    arrive(others(hist_y, ny), rsem.at[3])
    total_h = hist_y[0]
    for o in range(1, ny):
        total_h = total_h + hist_y[o]
    counts[my_xc] = total_h
    for ox, oc in xc_steps:
        send(counts.at[my_xc], counts.at[my_xc], ssem.at[4], rsem.at[4], peer(ox=ox, oc=oc))

    unit(0, ny - 2)
    swapped(ny - 1)
    unit(0, 4)
    for o in (3, ny - 3):
        for ox in xs:
            landed(o, ox)
            swap(o, ox)
    for o in far_y:
        swapped(o)
    for o in (3, ny - 3):
        unit(0, o)
    for o in (3, ny - 3):
        swapped(o)

    best = jnp.maximum(jnp.min(nearest[...], axis=0, keepdims=True) + norms, 0.0)
    mass = jnp.sum(best, axis=1, keepdims=True)

    def stage(buf, sem, devices, between):
        for o, device in enumerate(devices):
            send(buf.at[0], buf.at[o + 1], ssem.at[sem], rsem.at[sem], device)
        between()
        arrive(others(buf, len(devices) + 1), rsem.at[sem])
        return jnp.sum(buf[...], axis=0)

    targets = row * (K_FINAL // (nx * ny * CORES)) + lax.broadcasted_iota(I32, (16, 128), 0)
    state = {}

    def product(member, table):
        parts = jnp.concatenate(split3(member), axis=0)
        out = jnp.dot(parts, table, preferred_element_type=F32)
        return out[0:16] + out[16:32] + out[32:48]

    def lloyd_centres():
        arrive(others(counts, nxc), rsem.at[4])
        weights = 1.0 + jnp.concatenate([counts[q] for q in range(nxc)], axis=0)
        pieces = []
        for t in range(16):
            hit = jnp.broadcast_to(owner_ref[t:t + 1, :], (16, 128)) == targets
            pieces.append(jnp.where(hit, jnp.broadcast_to(weights[t:t + 1, :], (16, 128)), 0.0))
        den = pieces[0]
        for t in range(1, 16):
            den = den + pieces[t]
        state["weights"] = weights
        state["den"] = den
        state["num"] = product(jnp.concatenate(pieces, axis=1), cen[...])

    def lloyd_slots(c):
        weights = state["weights"]
        num, den = state["num"], state["den"]
        for ox in range(nx):
            for o in range(ny):
                tail = big[c, o, ox, rows - 8:rows + 8, :].astype(F32)
                meta[0, o:o + 1, :] = tail[8:9, 0:128]
                meta[1, o:o + 1, :] = tail[8:9, 128:256]
                meta[2, o:o + 1, :] = tail[9:10, 0:128]
            code = (meta[0] + meta[1] * 256.0 + meta[2] * 65536.0).astype(I32) - 1
            valid = code >= 0
            owner = jnp.where(valid, code & 1023, -1)
            ident = jnp.where(valid, code >> 10, 0)
            high = ident >> 7
            low = ident & 127
            weight = jnp.zeros((ny, 128), F32)
            for h in range(16):
                table = jnp.broadcast_to(weights[16 + h:17 + h, :], (ny, 128))
                got = jnp.take_along_axis(table, low, axis=1)
                weight = jnp.where(high == h, got, weight)
            lanes = lax.broadcasted_iota(I32, (ny, 128), 1)
            owner = jnp.where(lanes < rows, owner, -1)
            for o in range(ny):
                hit = jnp.broadcast_to(owner[o:o + 1, :], (16, 128)) == targets
                member = jnp.where(hit, jnp.broadcast_to(weight[o:o + 1, :], (16, 128)), 0.0)
                den = den + member
                num = num + product(member[:, :blk], big[c, o, ox])
        state["num"], state["den"] = num, den

    def lloyd_first():
        lloyd_centres()
        lloyd_slots(0)

    tot_p[0] = jnp.broadcast_to(mass, (1, 128))
    tot_z[0] = stage(tot_p, 5, plane_peers, lloyd_first)
    total = stage(tot_z, 7, [peer(oz=o) for o in range(1, nz)], lambda: lloyd_slots(1))
    den = jnp.sum(state["den"], axis=1, keepdims=True)
    final_ref[...] = state["num"] / den
    scaled = best * npts
    for b in range(8):
        cost_ref[b:b + 1, :] = scaled[:, b * 128:(b + 1) * 128] / total
    drain(others(zbuf, nz), ssem.at[0])
    drain(others(hist_x, nxc), ssem.at[1])
    drain(others(hist_z, nz), ssem.at[2])
    drain(others(hist_y, ny), ssem.at[3])
    drain(others(counts, nxc), ssem.at[4])
    drain(others(tot_p, nxc * ny), ssem.at[5])
    drain(others(tot_z, nz), ssem.at[7])
    drain(big.at[1], ssem.at[8])
    drain(big.at[0, 0, pl.ds(0, 3)], ssem.at[9])
    drain(big.at[0, pl.ds(0, 3)], ssem.at[10])
    drain(big.at[0, pl.ds(0, 4)], ssem.at[11])


def hand_over(cost_ref, final_ref, cost_out, final_out):
    cost_out[...] = cost_ref[...]
    final_out[...] = final_ref[...]


def shards(nx, ny, nz, points, centres, picks, assign_pts, cand_assign):
    nxc = nx * CORES
    blk = (nz * 2 * CAP + 2 + 15) // 16 * 16
    dma = pltpu.SemaphoreType.DMA
    per = 32 // nxc
    vmem = pl.BlockSpec(memory_space=pltpu.VMEM)
    hbm = pl.BlockSpec(memory_space=pltpu.MemorySpace.HBM)
    scratch = [
        pltpu.VMEM(picks.shape, I32), pltpu.VMEM((32, 128), I32), pltpu.VMEM((8, 128), I32),
        pltpu.VMEM((16, D), BF16),
        pltpu.VMEM(points.shape, BF16), pltpu.VMEM(points.shape, BF16),
        pltpu.VMEM(centres.shape, BF16), pltpu.VMEM((16, 128), I32),
        pltpu.VMEM((nz, 8, D), BF16), pltpu.VMEM((CORES, ny, nx, blk, D), BF16),
        pltpu.VMEM((8, 1024), F32), pltpu.VMEM((3, ny, 128), F32),
        pltpu.VMEM((nxc, per, 128), F32), pltpu.VMEM((nxc, per, 128), F32),
        pltpu.VMEM((nz, per, 128), F32), pltpu.VMEM((ny, per, 128), F32),
        pltpu.VMEM((nxc, per, 128), F32),
        pltpu.VMEM((nxc * ny, 1, 128), F32), pltpu.VMEM((nz, 1, 128), F32), dma((6,)),
    ]
    scratch += [dma((12,)), dma((8,)), dma((nx * ny,)), dma((ny,))]
    cost, final = pl.pallas_call(
        functools.partial(kernel, nx, ny, nz, float(1024 * nx * ny * CORES * nz)),
        out_shape=(jax.ShapeDtypeStruct((8, 128), F32), jax.ShapeDtypeStruct((16, D), F32)),
        in_specs=[hbm] * 5,
        out_specs=(vmem, vmem),
        scratch_shapes=scratch,
        compiler_params=pltpu.CompilerParams(
            collective_id=0, has_side_effects=True, vmem_limit_bytes=60 << 20),
    )(picks, cand_assign.reshape(32, 128), assign_pts.reshape(8, 128), points, centres)
    cost, final = pl.pallas_call(
        hand_over,
        out_shape=(jax.ShapeDtypeStruct((8, 128), F32), jax.ShapeDtypeStruct((16, D), F32)),
    )(cost, final)
    return cost.reshape(1024), final


def solution(mesh):
    nz = mesh.shape["col"]
    nx, ny = 4, mesh.shape["row"] // (4 * CORES)
    placed = (P(("row", "col"), None), P(), P(), P(("row", "col")), P())
    return jax.shard_map(
        functools.partial(shards, nx, ny, nz),
        mesh=mesh,
        in_specs=placed,
        out_specs=(P(("row", "col")), P("row", None)),
        check_vma=False,
    )
```

```python
import functools
import jax
import jax.numpy as jnp
from jax import lax
from jax.experimental import pallas as pl
from jax.experimental.pallas import tpu as pltpu
from jax.sharding import PartitionSpec as P

K_FINAL = 1024
CORES = 2
CAP = 3
D = 256
F32, BF16, I32 = jnp.float32, jnp.bfloat16, jnp.int32
MESH = pl.DeviceIdType.MESH
BIG = 3.0e38
FAR = 1 << 20


def split3(value):
    high = value.astype(BF16)
    rest = value - high.astype(F32)
    middle = rest.astype(BF16)
    low = (rest - middle.astype(F32)).astype(BF16)
    return high, middle, low


def contract_last(left, right):
    return lax.dot_general(left, right, (((1,), (1,)), ((), ())), preferred_element_type=F32)


def near_first(size):
    return sorted(range(1, size), key=lambda step: (min(step, size - step), step))


def kernel(nx, ny, nz, npts,
           picks_hbm, owner_hbm, assign_hbm, points_hbm, centres_hbm,
           cost_ref, final_ref,
           picks_ref, owner_ref, assign_ref, pts, pts2, cen, picked, zbuf, big, nearest, meta,
           hist, hist_x, hist_z, hist_y, counts,
           tot_p, tot_z, local_sem, ssem, rsem, block_sem, swap_sem):
    row = lax.axis_index("row")
    z = lax.axis_index("col")
    core = lax.rem(row, CORES)
    y = lax.rem(row // CORES, ny)
    x = row // (CORES * ny)
    me = row * nz + z
    slots = 2 * CAP
    rows = nz * slots
    blk = big.shape[3]
    nxc = nx * CORES

    def peer(ox=0, oy=0, oc=0, oz=0):
        px = lax.rem(x + ox, nx)
        py = lax.rem(y + oy, ny)
        pc = lax.rem(core + oc, CORES)
        return ((px * ny + py) * CORES + pc, lax.rem(z + oz, nz))

    def send(src, dst, out_sem, in_sem, device):
        pltpu.make_async_remote_copy(
            src_ref=src, dst_ref=dst, send_sem=out_sem, recv_sem=in_sem,
            device_id=device, device_id_type=MESH).start()

    def waiter(ref, sem):
        return pltpu.make_async_remote_copy(
            src_ref=ref, dst_ref=ref, send_sem=sem, recv_sem=sem,
            device_id=peer(oz=1), device_id_type=MESH)

    def arrive(ref, sem):
        waiter(ref, sem).wait_recv()

    def drain(ref, sem):
        waiter(ref, sem).wait_send()

    def others(ref, size):
        return ref.at[pl.ds(0, size - 1)]

    loads = [pltpu.make_async_copy(src, dst, local_sem.at[i]) for i, (src, dst) in enumerate(
        [(picks_hbm, picks_ref), (owner_hbm, owner_ref), (points_hbm, pts),
         (centres_hbm, cen), (assign_hbm, assign_ref)])]
    for load in loads:
        load.start()

    xc_steps = [(ox, oc) for ox in range(nx) for oc in range(CORES) if ox or oc]
    barrier = pltpu.get_barrier_semaphore()
    plane = [(ox, oy, oc) for ox in range(nx) for oy in range(ny) for oc in range(CORES)][1:]
    plane.sort(key=lambda p: -min(p[0], nx - p[0]) - min(p[1], ny - p[1]))
    plane_peers = [peer(ox=ox, oy=oy, oc=oc) for ox, oy, oc in plane]
    peers = [peer(oz=o) for o in range(1, nz)] + plane_peers
    for other in peers:
        pl.semaphore_signal(barrier, inc=1, device_id=other, device_id_type=MESH)

    loads[0].wait()
    loads[1].wait()
    for r in range(2):
        for b in range(8):
            picked[r * 8 + b:r * 8 + b + 1, :] = picks_ref[r:r + 1, b * 128:(b + 1) * 128]
    sub = lax.broadcasted_iota(I32, (8, 128), 0)
    lane = lax.broadcasted_iota(I32, (8, 128), 1)
    local_ids, codes = [], []
    for r in range(2):
        p = picked[r * 8:(r + 1) * 8, :]
        local = p - me * 1024
        own = (local >= 0) & (local < 1024)
        local = jnp.where(own, local, FAR)
        ids = r * 1024 + sub * 128 + lane
        code = ids * 1024 + owner_ref[16 + r * 8:24 + r * 8, :] + 1
        for s in range(CAP):
            first = jnp.min(jnp.min(local, axis=1, keepdims=True), axis=0, keepdims=True)
            hit = (local == first) & (local < FAR)
            coded = jnp.where(hit, code, 0)
            codes.append(jnp.max(jnp.max(coded, axis=1, keepdims=True), axis=0, keepdims=True))
            local_ids.append(first)
            local = jnp.where(local == first, FAR, local)
    slot_row = lax.broadcasted_iota(I32, (8, 1024), 0)
    point_lane = lax.broadcasted_iota(I32, (8, 1024), 1)
    want = jnp.full((8, 1024), FAR, I32)
    for s in range(slots):
        want = jnp.where(slot_row == s, local_ids[s], want)
    choose = jnp.where(want == point_lane, 1.0, 0.0)
    choose16 = jnp.concatenate([choose, jnp.zeros((8, 1024), F32)], axis=0).astype(BF16)
    lane1 = lax.broadcasted_iota(I32, (1, 128), 1)
    lane_dev = (lane1 * 43691) >> 18
    lane_slot = lane1 - lane_dev * slots
    code_row = jnp.zeros((1, 128), I32)
    for s in range(slots):
        code_row = jnp.where(lane_slot == s, codes[s], code_row)
    digit_a = (code_row & 255).astype(F32)
    digit_b = ((code_row >> 8) & 255).astype(F32)
    digit_c = (code_row >> 16).astype(F32)
    loads[2].wait()
    loads[3].wait()
    loads[4].wait()
    mine = jnp.dot(choose16, pts[...], preferred_element_type=F32)[:8, :]
    slot_col = lax.broadcasted_iota(I32, (8, D), 0)
    filled = jnp.zeros((8, D), I32)
    for s in range(slots):
        filled = jnp.where(slot_col == s, jnp.broadcast_to(local_ids[s], (8, D)), filled)
    spare = jnp.broadcast_to(cen[0:16, :].astype(F32)[0:1, :], (8, D))
    mine = jnp.where(filled >= FAR, spare, mine)
    row_six = jnp.concatenate([digit_a, digit_b], axis=1)
    row_seven = jnp.concatenate([digit_c, digit_c], axis=1)
    mine = jnp.where(slot_col == slots, jnp.broadcast_to(row_six, (8, D)), mine)
    mine = jnp.where(slot_col == slots + 1, jnp.broadcast_to(row_seven, (8, D)), mine)
    zbuf[z] = mine.astype(BF16)

    pl.semaphore_wait(barrier, len(peers))

    for o in near_first(nz)[::-1]:
        send(zbuf.at[z], zbuf.at[z], ssem.at[0], rsem.at[0], peer(oz=o))

    acc = jnp.zeros((32, 128), F32)
    hi_iota = lax.broadcasted_iota(I32, (32, 128), 0)
    lo_iota = lax.broadcasted_iota(I32, (128, 128), 0)
    for b in range(8):
        a = assign_ref[b:b + 1, :]
        left = jnp.where(hi_iota == (a >> 7), 1.0, 0.0).astype(BF16)
        right = jnp.where(lo_iota == (a & 127), 1.0, 0.0).astype(BF16)
        acc = acc + contract_last(left, right)
    per = 32 // nxc
    for q in range(nxc):
        hist[q] = acc[q * per:(q + 1) * per, :]
    my_xc = x * CORES + core
    for ox, oc in xc_steps:
        o = ox * CORES + oc
        target = lax.rem(x + ox, nx) * CORES + lax.rem(core + oc, CORES)
        send(hist.at[target], hist_x.at[o], ssem.at[1], rsem.at[1], peer(ox=ox, oc=oc))

    p32 = pts[...].astype(F32)
    pts2[...] = (p32 * -2.0).astype(BF16)
    square = p32 * p32
    square_hi = square.astype(BF16)
    square_lo = (square - square_hi.astype(F32)).astype(BF16)
    ones = jnp.ones((16, D), BF16)
    norms = (contract_last(ones, square_hi) + contract_last(ones, square_lo))[0:1, :]

    def fold(block, masked):
        b32 = block.astype(F32)
        norm = jnp.sum(b32 * b32, axis=1, keepdims=True)
        if masked:
            place = lax.rem(lax.broadcasted_iota(I32, norm.shape, 0), blk)
            norm = jnp.where(place < rows, norm, BIG)
        for part in range(4):
            q = slice(part * 256, (part + 1) * 256)
            d = contract_last(block, pts2[q, :]) + norm
            least = jnp.min(d.reshape(d.shape[0] // 8, 8, 256), axis=0)
            nearest[:, q] = jnp.minimum(nearest[:, q], least)

    nearest[...] = jnp.full(nearest.shape, BIG, F32)

    def fold_centres(i, carry):
        fold(cen[pl.ds(pl.multiple_of(i * 512, 512), 512), :], False)
        return carry

    lax.fori_loop(0, cen.shape[0] // 512, fold_centres, 0)

    arrive(others(zbuf, nz), rsem.at[0])
    column = jnp.concatenate([zbuf[i].astype(F32) for i in range(nz)], axis=0)
    crow = lax.broadcasted_iota(I32, column.shape, 0)
    clane = lax.broadcasted_iota(I32, column.shape, 1) & 127
    cdev = (clane * 43691) >> 18
    drop = ((crow & 7) >= slots) & ((crow >> 3) != cdev)
    column = jnp.where(drop, 0.0, column).astype(BF16)
    srow = lax.broadcasted_iota(I32, (blk, nz * 8), 0)
    scol = lax.broadcasted_iota(I32, (blk, nz * 8), 1)
    sdev = (srow * 43691) >> 18
    pick = (scol == sdev * 8 + (srow - sdev * slots)) & (srow < rows)
    pick = pick | ((srow == rows) & ((scol & 7) == slots))
    pick = pick | ((srow == rows + 1) & ((scol & 7) == slots + 1))
    packed = jnp.dot(jnp.where(pick, 1.0, 0.0).astype(BF16), column, preferred_element_type=F32)
    big[0, 0, 0] = packed.astype(BF16)

    xs = near_first(nx)
    near_x = (1, nx - 1)
    far_y = (2, ny - 2, 4)

    def slot(o, ox):
        return block_sem.at[o * nx + ox]

    def forward(o, ox, to_o, to_ox, out_sem, device):
        send(big.at[0, o, ox], big.at[0, to_o, to_ox], ssem.at[out_sem], slot(to_o, to_ox), device)

    def swap(o, ox):
        send(big.at[0, o, ox], big.at[1, o, ox], ssem.at[8], swap_sem.at[o], peer(oc=1))

    def sideways(o, ox):
        if o == 0 and ox in near_x:
            return
        if o == 0 or o == 2:
            forward(o, ox, o + 1, ox, 11, peer(oy=1))
        if o == 0 or o == ny - 2:
            forward(o, ox, (o + ny - 1) % ny, ox, 11, peer(oy=ny - 1))

    def across(o):
        for ox in xs:
            forward(o, 0, o, ox, 10, peer(ox=ox))

    def landed(o, ox):
        arrive(big.at[0, o, ox], slot(o, ox))

    def unit(c, o):
        fold(big[c, o].reshape(nx * blk, D), True)

    def swapped(o):
        arrive(big.at[1, o], swap_sem.at[o])
        unit(1, o)

    for o in far_y:
        forward(0, 0, o, 0, 9, peer(oy=o))
    across(0)
    sideways(0, 0)
    swap(0, 0)

    arrive(others(hist_x, nxc), rsem.at[1])
    total_h = hist[my_xc]
    for o in range(1, nxc):
        total_h = total_h + hist_x[o]
    hist_z[0] = total_h
    for o in range(1, nz):
        send(hist_z.at[0], hist_z.at[o], ssem.at[2], rsem.at[2], peer(oz=o))

    for o in (1, ny - 1):
        landed(o, 0)
        for ox in near_x:
            forward(o, 0, o, ox, 10, peer(ox=ox))
        swap(o, 0)
    for ox in xs:
        landed(0, ox)
        sideways(0, ox)
        swap(0, ox)
    for o in far_y:
        landed(o, 0)
        across(o)
        sideways(o, 0)
        swap(o, 0)
    unit(0, 0)

    arrive(others(hist_z, nz), rsem.at[2])
    total_h = hist_z[0]
    for o in range(1, nz):
        total_h = total_h + hist_z[o]
    hist_y[0] = total_h
    for o in range(1, ny):
        send(hist_y.at[0], hist_y.at[o], ssem.at[3], rsem.at[3], peer(oy=o))

    for o in (1, ny - 1):
        for ox in xs:
            landed(o, ox)
            swap(o, ox)
    swapped(0)
    for o in (3, ny - 3):
        landed(o, 0)
        swap(o, 0)
    unit(0, 1)
    for o in far_y[:2]:
        for ox in xs:
            landed(o, ox)
            sideways(o, ox)
            swap(o, ox)
    unit(0, ny - 1)
    for ox in xs:
        landed(4, ox)
        swap(4, ox)
    unit(0, 2)
    swapped(1)

    arrive(others(hist_y, ny), rsem.at[3])
    total_h = hist_y[0]
    for o in range(1, ny):
        total_h = total_h + hist_y[o]
    counts[my_xc] = total_h
    for ox, oc in xc_steps:
        send(counts.at[my_xc], counts.at[my_xc], ssem.at[4], rsem.at[4], peer(ox=ox, oc=oc))

    unit(0, ny - 2)
    swapped(ny - 1)
    unit(0, 4)
    for o in far_y:
        swapped(o)
    for o in (3, ny - 3):
        for ox in xs:
            landed(o, ox)
            swap(o, ox)
    for o in (3, ny - 3):
        unit(0, o)
    for o in (3, ny - 3):
        swapped(o)

    best = jnp.maximum(jnp.min(nearest[...], axis=0, keepdims=True) + norms, 0.0)
    mass = jnp.sum(best, axis=1, keepdims=True)

    def stage(buf, sem, devices, between):
        for o, device in enumerate(devices):
            send(buf.at[0], buf.at[o + 1], ssem.at[sem], rsem.at[sem], device)
        between()
        arrive(others(buf, len(devices) + 1), rsem.at[sem])
        return jnp.sum(buf[...], axis=0)

    targets = row * (K_FINAL // (nx * ny * CORES)) + lax.broadcasted_iota(I32, (16, 128), 0)
    state = {}

    def product(member, table):
        parts = jnp.concatenate(split3(member), axis=0)
        out = jnp.dot(parts, table, preferred_element_type=F32)
        return out[0:16] + out[16:32] + out[32:48]

    def lloyd_centres():
        arrive(others(counts, nxc), rsem.at[4])
        weights = 1.0 + jnp.concatenate([counts[q] for q in range(nxc)], axis=0)
        pieces = []
        for t in range(16):
            hit = jnp.broadcast_to(owner_ref[t:t + 1, :], (16, 128)) == targets
            pieces.append(jnp.where(hit, jnp.broadcast_to(weights[t:t + 1, :], (16, 128)), 0.0))
        den = pieces[0]
        for t in range(1, 16):
            den = den + pieces[t]
        state["weights"] = weights
        state["den"] = den
        state["num"] = product(jnp.concatenate(pieces, axis=1), cen[...])

    def lloyd_slots(c):
        weights = state["weights"]
        num, den = state["num"], state["den"]
        for ox in range(nx):
            for o in range(ny):
                tail = big[c, o, ox, rows - 8:rows + 8, :].astype(F32)
                meta[0, o:o + 1, :] = tail[8:9, 0:128]
                meta[1, o:o + 1, :] = tail[8:9, 128:256]
                meta[2, o:o + 1, :] = tail[9:10, 0:128]
            code = (meta[0] + meta[1] * 256.0 + meta[2] * 65536.0).astype(I32) - 1
            valid = code >= 0
            owner = jnp.where(valid, code & 1023, -1)
            ident = jnp.where(valid, code >> 10, 0)
            high = ident >> 7
            low = ident & 127
            weight = jnp.zeros((ny, 128), F32)
            for h in range(16):
                table = jnp.broadcast_to(weights[16 + h:17 + h, :], (ny, 128))
                got = jnp.take_along_axis(table, low, axis=1)
                weight = jnp.where(high == h, got, weight)
            lanes = lax.broadcasted_iota(I32, (ny, 128), 1)
            owner = jnp.where(lanes < rows, owner, -1)
            for o in range(ny):
                hit = jnp.broadcast_to(owner[o:o + 1, :], (16, 128)) == targets
                member = jnp.where(hit, jnp.broadcast_to(weight[o:o + 1, :], (16, 128)), 0.0)
                den = den + member
                num = num + product(member[:, :blk], big[c, o, ox])
        state["num"], state["den"] = num, den

    def lloyd_first():
        lloyd_centres()
        lloyd_slots(0)

    tot_p[0] = jnp.broadcast_to(mass, (1, 128))
    tot_z[0] = stage(tot_p, 5, plane_peers, lloyd_first)
    total = stage(tot_z, 7, [peer(oz=o) for o in range(1, nz)], lambda: lloyd_slots(1))
    den = jnp.sum(state["den"], axis=1, keepdims=True)
    final_ref[...] = state["num"] / den
    scaled = best * npts
    for b in range(8):
        cost_ref[b:b + 1, :] = scaled[:, b * 128:(b + 1) * 128] / total
    drain(others(zbuf, nz), ssem.at[0])
    drain(others(hist_x, nxc), ssem.at[1])
    drain(others(hist_z, nz), ssem.at[2])
    drain(others(hist_y, ny), ssem.at[3])
    drain(others(counts, nxc), ssem.at[4])
    drain(others(tot_p, nxc * ny), ssem.at[5])
    drain(others(tot_z, nz), ssem.at[7])
    drain(big.at[1], ssem.at[8])
    drain(big.at[0, 0, pl.ds(0, 3)], ssem.at[9])
    drain(big.at[0, pl.ds(0, 4)], ssem.at[10])
    drain(big.at[0, pl.ds(0, 3)], ssem.at[11])


def hand_over(cost_ref, final_ref, cost_out, final_out):
    cost_out[...] = cost_ref[...]
    final_out[...] = final_ref[...]


def shards(nx, ny, nz, points, centres, picks, assign_pts, cand_assign):
    nxc = nx * CORES
    blk = (nz * 2 * CAP + 2 + 15) // 16 * 16
    dma = pltpu.SemaphoreType.DMA
    per = 32 // nxc
    vmem = pl.BlockSpec(memory_space=pltpu.VMEM)
    hbm = pl.BlockSpec(memory_space=pltpu.MemorySpace.HBM)
    scratch = [
        pltpu.VMEM(picks.shape, I32), pltpu.VMEM((32, 128), I32), pltpu.VMEM((8, 128), I32),
        pltpu.VMEM(points.shape, BF16), pltpu.VMEM(points.shape, BF16),
        pltpu.VMEM(centres.shape, BF16), pltpu.VMEM((16, 128), I32),
        pltpu.VMEM((nz, 8, D), BF16), pltpu.VMEM((CORES, ny, nx, blk, D), BF16),
        pltpu.VMEM((8, 1024), F32), pltpu.VMEM((3, ny, 128), F32),
        pltpu.VMEM((nxc, per, 128), F32), pltpu.VMEM((nxc, per, 128), F32),
        pltpu.VMEM((nz, per, 128), F32), pltpu.VMEM((ny, per, 128), F32),
        pltpu.VMEM((nxc, per, 128), F32),
        pltpu.VMEM((nxc * ny, 1, 128), F32), pltpu.VMEM((nz, 1, 128), F32), dma((5,)),
    ]
    scratch += [dma((12,)), dma((8,)), dma((nx * ny,)), dma((ny,))]
    cost, final = pl.pallas_call(
        functools.partial(kernel, nx, ny, nz, float(1024 * nx * ny * CORES * nz)),
        out_shape=(jax.ShapeDtypeStruct((8, 128), F32), jax.ShapeDtypeStruct((16, D), F32)),
        in_specs=[hbm] * 5,
        out_specs=(vmem, vmem),
        scratch_shapes=scratch,
        compiler_params=pltpu.CompilerParams(
            collective_id=0, has_side_effects=True, vmem_limit_bytes=60 << 20),
    )(picks, cand_assign.reshape(32, 128), assign_pts.reshape(8, 128), points, centres)
    cost, final = pl.pallas_call(
        hand_over,
        out_shape=(jax.ShapeDtypeStruct((8, 128), F32), jax.ShapeDtypeStruct((16, D), F32)),
    )(cost, final)
    return cost.reshape(1024), final


def solution(mesh):
    nz = mesh.shape["col"]
    nx, ny = 4, mesh.shape["row"] // (4 * CORES)
    placed = (P(("row", "col"), None), P(), P(), P(("row", "col")), P())
    return jax.shard_map(
        functools.partial(shards, nx, ny, nz),
        mesh=mesh,
        in_specs=placed,
        out_specs=(P(("row", "col")), P("row", None)),
        check_vma=False,
    )
```
